32 devices in a mesh: scan: 2 (over y), ang: 4 (over z), row: 4 (over x, core).
Axes of the slice: x: 2, y: 2, z: 4, core: 2. Of those that a mesh axis runs over, the one named last changes fastest.
Arguments:
- raw_frames: bfloat16 [96, 128, 2560], P(('scan', 'ang'), 'row'), parts along dimension 0, may hold values from 0.099609375 to 1.5
- dark_field: bfloat16 [128, 2560], P('row'), may hold values from 0 to 0.079589844
- flat_field: bfloat16 [128, 2560], P('row'), may hold values from 0.796875 to 1.1953125
- kernel_taps: float32 [31], replicated, may hold values from 0.1 to 0.4
- partner: int32 [48], P('scan'), parts along dimension 0, may hold values from 24 to 47, as said below
- shifts: int32 [256], replicated, may hold values from -256 to 255, as said below
Outputs:
- sinograms: bfloat16 [96, 128, 2560], P('scan', ('ang', 'row')), parts along dimension 0
- correlation: float32 [256, 256], P(('scan', 'ang', 'row')), parts along dimension 0
The draws below stay inside these ranges and needn't reach their ends.
There are 2 independent parts, one for each index of `scan`. The reference program is written for one: setup_inputs(seed, part) draws one part's arguments, and reference() takes and returns one part's arrays. A program takes and returns all parts, laid end to end along the dimension named above; an argument that names none is the same for every part. Nothing has to cross between parts.
Inputs may be any that keep to these rules, and one draw needn't show every extreme that they name: partner[i] - i - 24 is -1, 0 or 1 for every i; partner[0] = 24 and partner[23] = 47. shifts[0] = -256 and shifts[255] = 255; values may repeat.
All inputs are finite; a program needn't handle non-finite values.
Results may differ from the reference program's by a relative error of at most 0.012.
The reference program's roundings to bfloat16 on the way (of `centered`, `ramp_kernel` and `mirrored`) count: a program that leaves them out, or rounds other values in their place, can miss the bound.
Values may be sent and summed in bfloat16 or wider, within the bound.
A program may use at most 128 MiB of HBM per device.

```python
import math
import jax
import jax.numpy as jnp
from jax import lax

C = 2560
TAPS = 31
SPAN = 256
NSHIFT = 256
NPROJ = 48
ROWS = 128
HALF = 24


def draw_partner(key, part):
    jitter = jax.random.randint(key, (NPROJ // 2,), -1, 2)
    position = jnp.arange(NPROJ // 2, dtype=jnp.int32)
    jitter = jnp.where(position == 0, 0, jitter)
    jitter = jnp.where(position == NPROJ // 2 - 1, 0, jitter)
    return (position + NPROJ // 2 + jitter).astype(jnp.int32)


def draw_shifts(key, part):
    values = jax.random.randint(key, (NSHIFT,), -SPAN, SPAN)
    position = jnp.arange(NSHIFT, dtype=jnp.int32)
    values = jnp.where(position == 0, -SPAN, values)
    values = jnp.where(position == NSHIFT - 1, SPAN - 1, values)
    return values.astype(jnp.int32)


def block_levels(rng, shape, cuts, smallest, largest):
    loudness, own = 1.0, jax.random.fold_in(rng, 6)
    for axis_at, blocks in cuts:
        draws = jnp.exp(jax.random.uniform(jax.random.fold_in(own, axis_at), (blocks,), jnp.float32, smallest / len(cuts), largest / len(cuts)))
        loudness = loudness * jnp.repeat(draws, shape[axis_at] // blocks).reshape([-1 if axis == axis_at else 1 for axis in range(len(shape))])
    return loudness


def setup_inputs(seed: int = 0, part: int = 0) -> dict:
    arg_keys = jax.random.split(jax.random.key(seed), 7)
    part_splits = jax.random.split(jax.random.fold_in(arg_keys[6], part), 7)
    return {
        "raw_frames": jnp.clip(0.099609375 + 1.4003906 * jax.random.uniform(part_splits[0], (NPROJ, ROWS, C), jnp.float32) ** block_levels(part_splits[0], (NPROJ, ROWS, C), ((0, 4), (1, 4)), -0.2, 0.2), 0.099609375, 1.5).astype(jnp.bfloat16),
        "dark_field": jnp.clip(0.079589844 * jax.random.uniform(arg_keys[1], (ROWS, C), jnp.float32) ** block_levels(arg_keys[1], (ROWS, C), ((0, 4),), -0.2, 0.2), 0.0, 0.079589844).astype(jnp.bfloat16),
        "flat_field": jnp.clip(0.796875 + 0.3984375 * jax.random.uniform(arg_keys[2], (ROWS, C), jnp.float32) ** block_levels(arg_keys[2], (ROWS, C), ((0, 4),), -0.2, 0.2), 0.796875, 1.1953125).astype(jnp.bfloat16),
        "kernel_taps": jnp.clip(jnp.exp(jax.random.uniform(arg_keys[3], (TAPS,), jnp.float32, math.log(0.1), math.log(0.4))), 0.1, 0.4),
        "partner": draw_partner(jax.random.fold_in(jax.random.fold_in(arg_keys[6], part), 71), part),
        "shifts": draw_shifts(jax.random.fold_in(arg_keys[6], 71), part),
    }


def absorb(raw_frames, dark_field, flat_field):
    counts = raw_frames.astype(jnp.float32)
    darkness = dark_field.astype(jnp.float32)
    brightness = flat_field.astype(jnp.float32)
    return -jnp.log((counts - darkness) / (brightness - darkness))


def column_pass(signal, kernel_taps):
    margin = kernel_taps.shape[0] // 2
    col_count = signal.shape[-1]
    padding = [(0, 0)] * (signal.ndim - 1) + [(margin, margin)]
    padded = jnp.pad(signal, padding)
    summed = kernel_taps[0] * padded[..., 0:col_count]
    for tap_index in range(1, kernel_taps.shape[0]):
        summed = summed + kernel_taps[tap_index] * padded[..., tap_index:tap_index + col_count]
    return summed


def row_pass(extended, kernel_taps, row_count, row_axis):
    summed = kernel_taps[0] * lax.slice_in_dim(extended, 0, row_count, axis=row_axis)
    for tap_index in range(1, kernel_taps.shape[0]):
        summed = summed + kernel_taps[tap_index] * lax.slice_in_dim(extended, tap_index, tap_index + row_count, axis=row_axis)
    return summed


def center_lines(lowpassed):
    return (lowpassed - jnp.mean(lowpassed, axis=-1, keepdims=True)).astype(jnp.bfloat16)


def ramp_matrix(col_count):
    distance = lax.iota(jnp.int32, col_count)[:, None] - lax.iota(jnp.int32, col_count)[None, :]
    spacing = distance.astype(jnp.float32)
    odd_distance = (distance % 2) != 0
    falloff = -4.0 / (math.pi * math.pi * jnp.maximum(spacing * spacing, 1.0))
    kernel = jnp.where(distance == 0, 1.0, jnp.where(odd_distance, falloff, 0.0))
    return kernel.astype(jnp.bfloat16)


def reference(raw_frames, dark_field, flat_field, kernel_taps, partner, shifts):
    margin = TAPS // 2
    ramp_kernel = ramp_matrix(C).astype(jnp.float32)

    def one_plane(frame_in):
        smooth = column_pass(absorb(frame_in, dark_field, flat_field), kernel_taps)
        extended = jnp.pad(smooth, ((margin, margin), (0, 0)))
        lowpassed = row_pass(extended, kernel_taps, ROWS, 0)
        centered = center_lines(lowpassed)
        filtered = jnp.dot(centered.astype(jnp.float32), ramp_kernel, precision=lax.Precision.HIGHEST)
        return centered, filtered.astype(jnp.bfloat16)

    centered, sinograms = lax.map(one_plane, raw_frames)
    factor = (HALF * C) ** -0.5

    def one_row(row_index):
        column = lax.dynamic_index_in_dim(centered, row_index, 1, False)
        leading = column[:HALF].astype(jnp.float32)
        mirrored = jnp.flip(jnp.take(column, partner, axis=0), axis=1).astype(jnp.float32)
        product = jnp.dot(leading.T, mirrored, precision=lax.Precision.HIGHEST)
        padded = jnp.pad(product, ((0, 0), (SPAN, SPAN)))
        window_width = C + 2 * SPAN
        flattened = jnp.pad(padded.reshape(-1), (0, C))
        skewed = flattened.reshape(C, window_width + 1)[:, :2 * SPAN]
        diagonal = jnp.sum(skewed, axis=0)
        return jnp.take(diagonal, shifts + SPAN) * factor

    correlation = lax.map(one_row, lax.iota(jnp.int32, ROWS))
    return sinograms, correlation
```

```python
import functools
import math

import jax
import jax.numpy as jnp
from jax import lax
from jax.experimental import pallas as pl
from jax.experimental.pallas import tpu as pltpu
from jax.sharding import PartitionSpec as P

SPAN = 256
LANES = 128
TILE = 256
CORES = 2
LAG = 3
MESH = pl.DeviceIdType.MESH


def split(value):
    high = value.astype(jnp.bfloat16)
    low = (value - high.astype(jnp.float32)).astype(jnp.bfloat16)
    return high, low


def band(taps_ref, lag):
    tap_count = taps_ref.shape[0]
    total = jnp.zeros(lag.shape, jnp.float32)
    for tap_index in range(tap_count):
        total = jnp.where(lag == tap_index, taps_ref[tap_index], total)
    return total


def dot(left, right):
    return jnp.dot(left, right, preferred_element_type=jnp.float32)


def ramp_block(offset):
    shape = (TILE, TILE)
    distance = (
        lax.broadcasted_iota(jnp.int32, shape, 0)
        - lax.broadcasted_iota(jnp.int32, shape, 1)
        + offset
    )
    spacing = distance.astype(jnp.float32)
    odd_distance = (distance & 1) != 0
    falloff = -4.0 / (math.pi * math.pi * jnp.maximum(spacing * spacing, 1.0))
    kernel = jnp.where(distance == 0, 1.0, jnp.where(odd_distance, falloff, 0.0))
    return kernel.astype(jnp.bfloat16)


def unpack(first, wide, planes, share, ang_count, lines_ref, x_ref, rows_ref):
    parts = x_ref.shape[0]
    size = wide * share
    for a in range(ang_count):
        start = a * planes + first
        for p in range(wide):
            line = lines_ref[start + p].astype(jnp.float32)
            for q in range(parts):
                x_ref[q, pl.ds((start + p) * share, share)] = line[:, q * LANES : (q + 1) * LANES]
        for q in range(parts):
            rows_ref[pl.ds(a * size, size), pl.ds(q * LANES, LANES)] = x_ref[
                q, pl.ds(start * share, size)
            ].astype(jnp.bfloat16)


def pair(first, end, planes, share, partner_ref, x_ref, left_ref, right_ref):
    parts, count, _ = x_ref.shape
    half = count // share // 2
    pad = SPAN // LANES
    width = end - first
    base = first * (half // planes)

    def pick(k, carry):
        a, p = k // width, k % width
        i = a * planes + (first + p + 1) % planes
        offset = partner_ref[i] - i - half
        middle = half + i

        def line(index):
            return x_ref[:, pl.ds(pl.multiple_of(index * share, share), share)]

        following = line(jnp.minimum(middle + 1, 2 * half - 1))
        chosen = jnp.where(offset > 0, following, line(middle))
        place = pl.ds(pl.multiple_of((base + k) * share, share), share)
        right_ref[pl.ds(pad, parts), place] = jnp.where(offset < 0, line(middle - 1), chosen)
        left_ref[:, place] = line(i)
        return carry

    lax.fori_loop(0, (half // planes) * width, pick, 0)


def products(r, first, end, planes, share, left_ref, right_ref):
    parts, count, _ = left_ref.shape
    pairs = count // share // planes
    pad = SPAN // LANES
    rows = pl.ds(first * pairs * share + r, (end - first) * pairs, stride=share)
    left = jnp.concatenate([left_ref[q, rows] for q in range(parts)], axis=0).astype(jnp.bfloat16)
    pieces = [right_ref[v, rows] for v in range(parts + 2 * pad)]
    last = parts - 1
    right = jnp.concatenate(
        [
            jnp.concatenate([pieces[last - q + v] for q in range(parts)], axis=0)
            for v in range(2 * pad + 1)
        ],
        axis=1,
    ).astype(jnp.bfloat16)
    return lax.dot_general(
        left, right, (((0,), (0,)), ((), ())), preferred_element_type=jnp.float32
    )


def correlate(cols, half, shifts_ref, corr_ref, prof_ref):
    lane = lax.broadcasted_iota(jnp.int32, (2 * SPAN, shifts_ref.shape[1]), 0)
    selector = (SPAN - 1 - lane == shifts_ref[...]).astype(jnp.float32)
    corr_ref[...] = jnp.dot(
        prof_ref[...],
        selector,
        precision=lax.Precision.HIGHEST,
        preferred_element_type=jnp.float32,
    ) * ((half * cols) ** -0.5)


def filter_kernel(
    sizes,
    taps_hbm,
    raw_hbm,
    dark_hbm,
    flat_hbm,
    partner_hbm,
    shifts_hbm,
    out_ref,
    corr_ref,
    taps_ref,
    partner_ref,
    shifts_ref,
    raw_ref,
    dark_ref,
    flat_ref,
    lines_ref,
    halo_ref,
    level_ref,
    dark_ext,
    gain_ext,
    row_band,
    col_band,
    x_cat,
    z_high,
    z_low,
    low_ref,
    send_ref,
    relay_ref,
    strip_ref,
    x_ref,
    rows_ref,
    left_ref,
    right_ref,
    prod_ref,
    prof_ref,
    tall_ref,
    acc_ref,
    out_stage,
    raw_sem,
    field_sem,
    write_sem,
    level_send,
    level_recv,
    halo_send,
    halo_recv,
    out_send,
    out_recv,
    relay_send,
    relay_recv,
):
    ang_count, row_devices, halo, plan = sizes
    planes, rows, cols = raw_ref.shape
    margin = taps_ref.shape[0] // 2
    dests, _, share, _ = send_ref.shape
    ext = rows + 2 * halo
    tiles = cols // TILE
    blocks = 2 * tiles - 1
    scan, ang, row = lax.axis_index("scan"), lax.axis_index("ang"), lax.axis_index("row")
    has = (row > 0, row < row_devices - 1)
    peer = (jnp.maximum(row - 1, 0), jnp.minimum(row + 1, row_devices - 1))

    def raw_copy(g):
        return pltpu.make_async_copy(raw_hbm.at[g], raw_ref.at[g], raw_sem.at[g])

    fields = (
        (taps_hbm, taps_ref),
        (dark_hbm, dark_ref),
        (flat_hbm, flat_ref),
        (partner_hbm, partner_ref),
        (shifts_hbm, shifts_ref),
    )

    def field_copy(which):
        source, target = fields[which]
        return pltpu.make_async_copy(source, target, field_sem.at[which])

    for which in range(len(fields)):
        field_copy(which).start()

    def fetch(g, carry):
        raw_copy(g).start()
        return carry

    lax.fori_loop(0, planes, fetch, 0)

    barrier = pltpu.get_barrier_semaphore()
    for a in range(ang_count):
        for b in range(row_devices):

            @pl.when(jnp.logical_or(ang != a, row != b))
            def _():
                pl.semaphore_signal(barrier, inc=1, device_id=(scan, a, b), device_id_type=MESH)

    field_copy(0).wait()
    r_out = lax.broadcasted_iota(jnp.int32, (rows, ext), 0)
    r_in = lax.broadcasted_iota(jnp.int32, (rows, ext), 1)
    high, low = split(band(taps_ref, r_in - r_out - (halo - margin)))
    row_band[:rows, :ext] = high
    row_band[:rows, ext:] = high
    row_band[rows:, :ext] = low
    row_band[rows:, ext:] = jnp.zeros((rows, ext), jnp.bfloat16)
    c_in = lax.broadcasted_iota(jnp.int32, (TILE + 2 * LANES, TILE), 0)
    c_out = lax.broadcasted_iota(jnp.int32, (TILE + 2 * LANES, TILE), 1)
    high, low = split(band(taps_ref, c_in - c_out - (LANES - margin)))
    col_band[:, :TILE] = high
    col_band[:, TILE:] = low
    for z_ref in (z_high, z_low):
        z_ref[:, :LANES] = jnp.zeros((rows, LANES), jnp.bfloat16)
        z_ref[:, LANES + cols :] = jnp.zeros((rows, LANES), jnp.bfloat16)

    for which in range(1, len(fields)):
        field_copy(which).wait()

    def wait_raw(g, carry):
        raw_copy(g).wait()
        return carry

    lax.fori_loop(0, planes, wait_raw, 0)
    pl.semaphore_wait(barrier, ang_count * row_devices - 1)

    def level_copy(side, which):
        source = (dark_ref, flat_ref)[which]
        start = 0 if side == 0 else rows - halo
        return pltpu.make_async_remote_copy(
            src_ref=source.at[pl.ds(start, halo)],
            dst_ref=level_ref.at[1 - side, which],
            send_sem=level_send.at[side, which],
            recv_sem=level_recv.at[1 - side, which],
            device_id=(scan, ang, peer[side]),
            device_id_type=MESH,
        )

    def halo_copy(side, g):
        start = 0 if side == 0 else rows - halo
        return pltpu.make_async_remote_copy(
            src_ref=raw_ref.at[g, pl.ds(start, halo)],
            dst_ref=halo_ref.at[1 - side, g],
            send_sem=halo_send.at[side],
            recv_sem=halo_recv.at[1 - side, g],
            device_id=(scan, ang, peer[side]),
            device_id_type=MESH,
        )

    def start_halo(g):
        for side in range(2):

            @pl.when(has[side])
            def _():
                halo_copy(side, g).start()

    for side in range(2):

        @pl.when(has[side])
        def _():
            for which in range(2):
                level_copy(side, which).start()

    for g in range(2):
        start_halo(g)

    def levels(dark, flat):
        dark = dark.astype(jnp.float32)
        return dark, jnp.log(flat.astype(jnp.float32) - dark)

    dark_ext[pl.ds(halo, rows)], gain_ext[pl.ds(halo, rows)] = levels(dark_ref[...], flat_ref[...])
    for side in range(2):

        @pl.when(has[side])
        def _():
            for which in range(2):
                level_copy(1 - side, which).wait_recv()

        at = 0 if side == 0 else halo + rows
        dark_ext[pl.ds(at, halo)], gain_ext[pl.ds(at, halo)] = levels(
            level_ref[side, 0], level_ref[side, 1]
        )

    upper = dests // row_devices

    def target(d):
        return upper * row + d // row_devices, d % row_devices

    def is_self(d):
        a, b = target(d)
        return jnp.logical_and(a == ang, b == row)

    def is_relayed(d):
        a, b = target(d)
        return jnp.logical_and(a != ang, b // CORES != row // CORES)

    def place(a, g):
        return lines_ref.at[a * planes + g]

    def out_copy(d, g):
        a, b = target(d)
        return pltpu.make_async_remote_copy(
            src_ref=send_ref.at[d, g],
            dst_ref=place(ang, g),
            send_sem=out_send.at[d],
            recv_sem=out_recv.at[ang, g],
            device_id=(scan, a, b),
            device_id_type=MESH,
        )

    def first_hop(d, g):
        return pltpu.make_async_remote_copy(
            src_ref=send_ref.at[d, g],
            dst_ref=relay_ref.at[row, d // row_devices, g],
            send_sem=out_send.at[d],
            recv_sem=relay_recv.at[row, d // row_devices, g],
            device_id=(scan, ang, d % row_devices),
            device_id_type=MESH,
        )

    def second_hop(b, u, g):
        return pltpu.make_async_remote_copy(
            src_ref=relay_ref.at[b, u, g],
            dst_ref=place(ang, g),
            send_sem=relay_send.at[b, u],
            recv_sem=out_recv.at[ang, g],
            device_id=(scan, upper * b + u, row),
            device_id_type=MESH,
        )

    def own_copy(d, g):
        return pltpu.make_async_copy(send_ref.at[d, g], place(ang, g), out_recv.at[ang, g])

    def relays(b, u):
        return jnp.logical_and(b // CORES != row // CORES, upper * b + u != ang)

    inner = range(1, row_devices - 1)
    outer = (0, row_devices - 1)

    def relay(sources, g):
        for b in sources:
            for u in range(upper):

                @pl.when(relays(b, u))
                def _():
                    arrived = relay_ref.at[b, u, g]
                    pltpu.make_async_copy(arrived, arrived, relay_recv.at[b, u, g]).wait()
                    second_hop(b, u, g).start()

    def send(g):
        for d in range(dests):

            @pl.when(is_relayed(d))
            def _():
                first_hop(d, g).start()

        for d in range(dests):

            @pl.when(is_self(d))
            def _():
                own_copy(d, g).start()

            @pl.when(jnp.logical_not(jnp.logical_or(is_relayed(d), is_self(d))))
            def _():
                out_copy(d, g).start()

    step = cols // 2 if cols // 2 % TILE == 0 else TILE

    def lowpass(g):
        def put(at, counts, valid):
            size = counts.shape[0]
            value = gain_ext[pl.ds(at, size)] - jnp.log(
                counts.astype(jnp.float32) - dark_ext[pl.ds(at, size)]
            )
            if valid is not None:
                value = jnp.where(valid, value, 0.0)
            high, low = split(value)
            x_cat[pl.ds(at, size)] = high
            x_cat[pl.ds(ext + at, size)] = low

        put(0, halo_ref[0, g], has[0])
        put(halo, raw_ref[g], None)
        put(halo + rows, halo_ref[1, g], has[1])

        def row_pass(n, carry):
            at = pl.multiple_of(n * step, TILE)
            both = dot(row_band[...], x_cat[:, pl.ds(at, step)])
            high, low = split(both[:rows] + both[rows:])
            to = pl.multiple_of(n * step + LANES, LANES)
            z_high[:, pl.ds(to, step)] = high
            z_low[:, pl.ds(to, step)] = low
            return carry

        lax.fori_loop(0, cols // step, row_pass, 0)

        def windows(z_ref):
            return jnp.concatenate(
                [z_ref[:, n * TILE : (n + 1) * TILE + 2 * LANES] for n in range(tiles)], axis=0
            )

        both = dot(windows(z_high), col_band[...])
        rest = dot(windows(z_low), col_band[:, :TILE])
        value = both[:, :TILE] + (both[:, TILE:] + rest)
        total = jnp.zeros((rows, 1), jnp.float32)
        for n in range(tiles):
            tile = value[n * rows : (n + 1) * rows]
            low_ref[:, n * TILE : (n + 1) * TILE] = tile
            total = total + jnp.sum(tile, axis=1, keepdims=True)
        mean = total * (1.0 / cols)
        for d in range(dests):
            at = d * share
            send_ref[d, g] = (low_ref[pl.ds(at, share)] - mean[at : at + share]).astype(
                jnp.bfloat16
            )

    def build(n, carry):
        base = pl.multiple_of(n * TILE, TILE)
        strip_ref[pl.ds(base, TILE)] = ramp_block(base - (tiles - 1) * TILE)
        return carry

    def advance(g, carry):
        for side in range(2):

            @pl.when(has[side])
            def _():
                halo_copy(1 - side, g).wait_recv()

        lowpass(g)
        send(g)

        @pl.when(g + 2 < planes)
        def _():
            start_halo(g + 2)

        each = -(-blocks // (planes - 1))
        lax.fori_loop(jnp.minimum(g * each, blocks), jnp.minimum((g + 1) * each, blocks), build, 0)

        @pl.when(g > 0)
        def _():
            relay(outer, g - 1)

        @pl.when(g >= LAG)
        def _():
            relay(inner, g - LAG)

        return carry

    def arrive(first, wide):
        for g in range(first, first + wide):
            for a in range(ang_count):
                here = place(a, g)
                pltpu.make_async_copy(here, here, out_recv.at[a, g]).wait()

    def sinogram(first, wide):
        arrive(first, wide)
        unpack(first, wide, planes, share, ang_count, lines_ref, x_ref, rows_ref)
        size = wide * share
        count = ang_count * size

        def ramp(n, carry):
            start = pl.multiple_of((tiles - 1 - n) * TILE, TILE)
            value = dot(rows_ref[:count], strip_ref[pl.ds(start, cols)])
            at = pl.ds(pl.multiple_of(n * TILE, TILE), TILE)
            for a in range(ang_count):
                for p in range(wide):
                    own = a * size + p * share
                    out_stage[a * planes + first + p, :, at] = value[own : own + share].astype(
                        jnp.bfloat16
                    )
            return carry

        lax.fori_loop(0, tiles, ramp, 0)
        for a in range(ang_count):
            write(a, first, wide).start()

    def last_sinogram(first, wide):
        arrive(first, wide)
        unpack(first, wide, planes, share, ang_count, lines_ref, x_ref, rows_ref)
        size = wide * share
        count = ang_count * size
        for k in range(tiles):
            tall_ref[k * count : (k + 1) * count] = rows_ref[:count, k * TILE : (k + 1) * TILE]
        for shift in sorted(range(1 - tiles, tiles), key=abs):
            low, high = max(0, shift), min(tiles, tiles + shift)
            block = strip_ref[(tiles - 1 + shift) * TILE : (tiles + shift) * TILE]
            value = dot(tall_ref[low * count : high * count], block)
            here = pl.ds((low - shift) * count, (high - low) * count)
            if shift:
                acc_ref[here] += value
            else:
                acc_ref[here] = value
        for n in range(tiles):
            for a in range(ang_count):
                for p in range(wide):
                    own = n * count + a * size + p * share
                    out_stage[a * planes + first + p, :, n * TILE : (n + 1) * TILE] = acc_ref[
                        own : own + share
                    ].astype(jnp.bfloat16)
        for a in range(ang_count):
            write(a, first, wide).start()

    def write(a, first, wide):
        here = pl.ds(a * planes + first, wide)
        return pltpu.make_async_copy(out_stage.at[here], out_ref.at[here], write_sem.at[a, first])

    pairs, early = ang_count * planes // 2, planes * 2 // 3
    pad = SPAN // LANES
    done, chunks, joined = 0, [], False
    for until, first, wide in plan:
        if until > done:
            lax.fori_loop(done, until, advance, 0)
            done = until
            if until == planes:
                for g in range(planes - LAG, planes):
                    relay(inner, g)
                relay(outer, planes - 1)
                for v in range(pad):
                    right_ref[v] = jnp.zeros(right_ref.shape[1:], jnp.float32)
                    right_ref[pad + cols // LANES + v] = jnp.zeros(right_ref.shape[1:], jnp.float32)
        if first + wide == planes:
            last_sinogram(first, wide)
        else:
            sinogram(first, wide)
        chunks.append((first, wide))
        if first + wide > early + 1 and not joined:
            joined = True
            pair(0, early, planes, share, partner_ref, x_ref, left_ref, right_ref)
            for r in range(share):
                prod_ref[r] = products(r, 0, early, planes, share, left_ref, right_ref)

    pair(early, planes, planes, share, partner_ref, x_ref, left_ref, right_ref)
    for r in range(share):
        product = prod_ref[r] + products(r, early, planes, planes, share, left_ref, right_ref)
        skewed = pltpu.roll(product, 0, 1, stride=1, stride_axis=0)
        prof_ref[pl.ds(r, 1)] = jnp.sum(skewed, axis=0, keepdims=True)[:, LANES:]
    correlate(cols, pairs, shifts_ref, corr_ref, prof_ref)

    for first, wide in chunks:
        for a in range(ang_count):
            write(a, first, wide).wait()

    for d in range(dests):

        @pl.when(jnp.logical_not(is_self(d)))
        def _():
            sent = send_ref.at[d]
            pltpu.make_async_copy(sent, sent, out_send.at[d]).wait()

    for b in range(row_devices):
        for u in range(upper):

            @pl.when(relays(b, u))
            def _():
                sent = relay_ref.at[b, u]
                pltpu.make_async_copy(sent, sent, relay_send.at[b, u]).wait()

    for side in range(2):

        @pl.when(has[side])
        def _():
            sent = halo_ref.at[side]
            pltpu.make_async_copy(sent, sent, halo_send.at[side]).wait()

    for side in range(2):

        @pl.when(has[side])
        def _():
            for which in range(2):
                level_copy(side, which).wait_send()


def schedule(planes):
    wide = max(planes // 3, 1)
    return (
        (planes - wide, 0, wide),
        (planes, wide, wide),
        (planes, 2 * wide, planes - 2 * wide - 1),
        (planes, planes - 1, 1),
    )


def emit_kernel(sino_ref, corr_ref, sino_out, corr_out, sems):
    a = pltpu.make_async_copy(sino_ref, sino_out, sems.at[0])
    b = pltpu.make_async_copy(corr_ref, corr_out, sems.at[1])
    a.start()
    b.start()
    a.wait()
    b.wait()


def emit(sino, corr):
    hbm = pl.BlockSpec(memory_space=pl.ANY)
    return pl.pallas_call(
        emit_kernel,
        out_shape=(jax.ShapeDtypeStruct(sino.shape, sino.dtype), jax.ShapeDtypeStruct(corr.shape, corr.dtype)),
        in_specs=[hbm, hbm],
        out_specs=(hbm, hbm),
        scratch_shapes=[pltpu.SemaphoreType.DMA((2,))],
        compiler_params=pltpu.CompilerParams(vmem_limit_bytes=2**20),
    )(sino, corr)


def shards(raw_frames, dark_field, flat_field, kernel_taps, partner, shifts):
    planes, rows, cols = raw_frames.shape
    ang_count, row_devices = lax.axis_size("ang"), lax.axis_size("row")
    share = rows // ang_count
    margin = kernel_taps.shape[0] // 2
    halo = -(-margin // 16) * 16
    ext = rows + 2 * halo
    count, half = ang_count * planes, ang_count * planes // 2
    plan = schedule(planes)
    widest = max(wide for _, _, wide in plan)
    vmem = pl.BlockSpec(memory_space=pltpu.VMEM)
    smem = pl.BlockSpec(memory_space=pltpu.SMEM)
    hbm = pl.BlockSpec(memory_space=pl.ANY)
    bf16, f32 = jnp.bfloat16, jnp.float32
    dma = pltpu.SemaphoreType.DMA
    lines, corr = pl.pallas_call(
        functools.partial(filter_kernel, (ang_count, row_devices, halo, plan)),
        out_shape=(
            jax.ShapeDtypeStruct((count, share, cols), bf16),
            jax.ShapeDtypeStruct((share, shifts.shape[0]), f32),
        ),
        in_specs=[pl.BlockSpec(memory_space=pltpu.HBM)] * 6,
        out_specs=(hbm, vmem),
        scratch_shapes=[
            pltpu.SMEM(kernel_taps.shape, f32),
            pltpu.SMEM(partner.shape, jnp.int32),
            pltpu.VMEM((1,) + shifts.shape, jnp.int32),
            pltpu.VMEM((planes, rows, cols), bf16),
            pltpu.VMEM((rows, cols), bf16),
            pltpu.VMEM((rows, cols), bf16),
            pltpu.VMEM((count, share, cols), bf16),
            pltpu.VMEM((2, planes, halo, cols), bf16),
            pltpu.VMEM((2, 2, halo, cols), bf16),
            pltpu.VMEM((ext, cols), f32),
            pltpu.VMEM((ext, cols), f32),
            pltpu.VMEM((2 * rows, 2 * ext), bf16),
            pltpu.VMEM((TILE + 2 * LANES, 2 * TILE), bf16),
            pltpu.VMEM((2 * ext, cols), bf16),
            pltpu.VMEM((rows, cols + 2 * LANES), bf16),
            pltpu.VMEM((rows, cols + 2 * LANES), bf16),
            pltpu.VMEM((rows, cols), f32),
            pltpu.VMEM((ang_count, planes, share, cols), bf16),
            pltpu.VMEM((row_devices, ang_count // row_devices, planes, share, cols), bf16),
            pltpu.VMEM((2 * cols - TILE, TILE), bf16),
            pltpu.VMEM((cols // LANES, count * share, LANES), f32),
            pltpu.VMEM((ang_count * widest * share, cols), bf16),
            pltpu.VMEM((cols // LANES, half * share, LANES), f32),
            pltpu.VMEM(((cols + 2 * SPAN) // LANES, half * share, LANES), f32),
            pltpu.VMEM((share, LANES, 2 * SPAN + LANES), f32),
            pltpu.VMEM((share, 2 * SPAN), f32),
            pltpu.VMEM((cols // TILE * ang_count * share, TILE), bf16),
            pltpu.VMEM((cols // TILE * ang_count * share, TILE), f32),
            pltpu.VMEM((count, share, cols), bf16),
            dma((planes,)),
            dma((5,)),
            dma((ang_count, planes)),
            dma((2, 2)),
            dma((2, 2)),
            dma((2,)),
            dma((2, planes)),
            dma((ang_count,)),
            dma((ang_count, planes)),
            dma((row_devices, ang_count // row_devices)),
            dma((row_devices, ang_count // row_devices, planes)),
        ],
        compiler_params=pltpu.CompilerParams(collective_id=0, has_side_effects=True, vmem_limit_bytes=40 * 2**20),
    )(*(pltpu.with_memory_space_constraint(v, pltpu.HBM) for v in (kernel_taps, raw_frames, dark_field, flat_field, partner, shifts[None])))
    return emit(lines, corr)


def solution(mesh):
    in_specs = (
        P(("scan", "ang"), "row", None),
        P("row", None),
        P("row", None),
        P(),
        P("scan"),
        P(),
    )
    out_specs = (P("scan", ("ang", "row"), None), P(("scan", "ang", "row"), None))
    return jax.shard_map(shards, mesh=mesh, in_specs=in_specs, out_specs=out_specs, check_vma=False)
```

```python
import functools
import math

import jax
import jax.numpy as jnp
from jax import lax
from jax.experimental import pallas as pl
from jax.experimental.pallas import tpu as pltpu
from jax.sharding import PartitionSpec as P

SPAN = 256
LANES = 128
TILE = 256
CORES = 2
HOLD = 2
BEHIND = 5
AHEAD = 2
EXTRA = 0
MESH = pl.DeviceIdType.MESH


def split(value):
    high = value.astype(jnp.bfloat16)
    low = (value - high.astype(jnp.float32)).astype(jnp.bfloat16)
    return high, low


def band(taps_ref, lag):
    tap_count = taps_ref.shape[0]
    total = jnp.zeros(lag.shape, jnp.float32)
    for tap_index in range(tap_count):
        total = jnp.where(lag == tap_index, taps_ref[tap_index], total)
    return total


def dot(left, right):
    return jnp.dot(left, right, preferred_element_type=jnp.float32)


def ramp_block(offset):
    shape = (TILE, TILE)
    distance = (
        lax.broadcasted_iota(jnp.int32, shape, 0)
        - lax.broadcasted_iota(jnp.int32, shape, 1)
        + offset
    )
    spacing = distance.astype(jnp.float32)
    odd_distance = (distance & 1) != 0
    falloff = -4.0 / (math.pi * math.pi * jnp.maximum(spacing * spacing, 1.0))
    kernel = jnp.where(distance == 0, 1.0, jnp.where(odd_distance, falloff, 0.0))
    return kernel.astype(jnp.bfloat16)


def pair(first, end, planes, share, partner_ref, x_ref, left_ref, right_ref):
    parts, count, _ = x_ref.shape
    half = count // share // 2
    pad = SPAN // LANES
    width = end - first
    base = first * (half // planes)

    def pick(k, carry):
        a, p = k // width, k % width
        i = a * planes + (first + p + 1) % planes
        offset = partner_ref[i] - i - half
        middle = half + i

        def line(index):
            return x_ref[:, pl.ds(pl.multiple_of(index * share, share), share)]

        following = line(jnp.minimum(middle + 1, 2 * half - 1))
        chosen = jnp.where(offset > 0, following, line(middle))
        place = pl.ds(pl.multiple_of((base + k) * share, share), share)
        right_ref[pl.ds(pad, parts), place] = jnp.where(offset < 0, line(middle - 1), chosen)
        left_ref[:, place] = line(i)
        return carry

    lax.fori_loop(0, (half // planes) * width, pick, 0)


def products(r, first, end, planes, share, left_ref, right_ref):
    parts, count, _ = left_ref.shape
    pairs = count // share // planes
    pad = SPAN // LANES
    rows = pl.ds(first * pairs * share + r, (end - first) * pairs, stride=share)
    left = jnp.concatenate([left_ref[q, rows] for q in range(parts)], axis=0).astype(jnp.bfloat16)
    pieces = [right_ref[v, rows] for v in range(parts + 2 * pad)]
    last = parts - 1
    right = jnp.concatenate(
        [
            jnp.concatenate([pieces[last - q + v] for q in range(parts)], axis=0)
            for v in range(2 * pad + 1)
        ],
        axis=1,
    ).astype(jnp.bfloat16)
    return lax.dot_general(
        left, right, (((0,), (0,)), ((), ())), preferred_element_type=jnp.float32
    )


def correlate(cols, half, shifts_ref, corr_ref, prof_ref):
    lane = lax.broadcasted_iota(jnp.int32, (2 * SPAN, shifts_ref.shape[1]), 0)
    selector = (SPAN - 1 - lane == shifts_ref[...]).astype(jnp.float32)
    corr_ref[...] = jnp.dot(
        prof_ref[...],
        selector,
        precision=lax.Precision.HIGHEST,
        preferred_element_type=jnp.float32,
    ) * ((half * cols) ** -0.5)


def filter_kernel(
    sizes,
    taps_hbm,
    raw_hbm,
    dark_hbm,
    flat_hbm,
    partner_hbm,
    shifts_hbm,
    out_ref,
    corr_ref,
    taps_ref,
    partner_ref,
    shifts_ref,
    raw_ref,
    dark_ref,
    flat_ref,
    lines_ref,
    halo_ref,
    level_ref,
    dark_ext,
    gain_ext,
    row_band,
    col_band,
    x_cat,
    z_high,
    z_low,
    low_ref,
    send_ref,
    relay_ref,
    strip_ref,
    x_ref,
    left_ref,
    right_ref,
    prod_ref,
    prof_ref,
    tall_ref,
    acc_ref,
    out_stage,
    raw_sem,
    field_sem,
    write_sem,
    level_send,
    level_recv,
    halo_send,
    halo_recv,
    out_send,
    out_recv,
    relay_send,
    relay_recv,
):
    ang_count, row_devices, halo = sizes
    planes, rows, cols = raw_ref.shape
    margin = taps_ref.shape[0] // 2
    dests, _, share, _ = send_ref.shape
    ext = rows + 2 * halo
    tiles = cols // TILE
    blocks = 2 * tiles - 1
    scan, ang, row = lax.axis_index("scan"), lax.axis_index("ang"), lax.axis_index("row")
    has = (row > 0, row < row_devices - 1)
    peer = (jnp.maximum(row - 1, 0), jnp.minimum(row + 1, row_devices - 1))

    def raw_copy(g):
        return pltpu.make_async_copy(raw_hbm.at[g], raw_ref.at[g], raw_sem.at[g])

    fields = (
        (taps_hbm, taps_ref),
        (dark_hbm, dark_ref),
        (flat_hbm, flat_ref),
        (partner_hbm, partner_ref),
        (shifts_hbm, shifts_ref),
    )

    def field_copy(which):
        source, target = fields[which]
        return pltpu.make_async_copy(source, target, field_sem.at[which])

    for which in range(len(fields)):
        field_copy(which).start()

    def fetch(g, carry):
        raw_copy(g).start()
        return carry

    lax.fori_loop(0, planes, fetch, 0)

    barrier = pltpu.get_barrier_semaphore()
    for a in range(ang_count):
        for b in range(row_devices):

            @pl.when(jnp.logical_or(ang != a, row != b))
            def _():
                pl.semaphore_signal(barrier, inc=1, device_id=(scan, a, b), device_id_type=MESH)

    field_copy(0).wait()
    r_out = lax.broadcasted_iota(jnp.int32, (rows, ext), 0)
    r_in = lax.broadcasted_iota(jnp.int32, (rows, ext), 1)
    high, low = split(band(taps_ref, r_in - r_out - (halo - margin)))
    row_band[:rows, :ext] = high
    row_band[:rows, ext:] = high
    row_band[rows:, :ext] = low
    row_band[rows:, ext:] = jnp.zeros((rows, ext), jnp.bfloat16)
    c_in = lax.broadcasted_iota(jnp.int32, (TILE + 2 * LANES, TILE), 0)
    c_out = lax.broadcasted_iota(jnp.int32, (TILE + 2 * LANES, TILE), 1)
    high, low = split(band(taps_ref, c_in - c_out - (LANES - margin)))
    col_band[:, :TILE] = high
    col_band[:, TILE:] = low
    for z_ref in (z_high, z_low):
        z_ref[:, :LANES] = jnp.zeros((rows, LANES), jnp.bfloat16)
        z_ref[:, LANES + cols :] = jnp.zeros((rows, LANES), jnp.bfloat16)

    for which in range(1, len(fields)):
        field_copy(which).wait()

    pl.semaphore_wait(barrier, ang_count * row_devices - 1)

    def level_copy(side, which):
        source = (dark_ref, flat_ref)[which]
        start = 0 if side == 0 else rows - halo
        return pltpu.make_async_remote_copy(
            src_ref=source.at[pl.ds(start, halo)],
            dst_ref=level_ref.at[1 - side, which],
            send_sem=level_send.at[side, which],
            recv_sem=level_recv.at[1 - side, which],
            device_id=(scan, ang, peer[side]),
            device_id_type=MESH,
        )

    def halo_copy(side, g):
        start = 0 if side == 0 else rows - halo
        return pltpu.make_async_remote_copy(
            src_ref=raw_ref.at[g, pl.ds(start, halo)],
            dst_ref=halo_ref.at[1 - side, g],
            send_sem=halo_send.at[side],
            recv_sem=halo_recv.at[1 - side, g],
            device_id=(scan, ang, peer[side]),
            device_id_type=MESH,
        )

    far = (row % CORES == 0, row % CORES == CORES - 1)

    def start_halo(g, distant):
        for side in range(2):

            @pl.when(jnp.logical_and(has[side], far[side] == distant))
            def _():
                halo_copy(side, g).start()

    for side in range(2):

        @pl.when(has[side])
        def _():
            for which in range(2):
                level_copy(side, which).start()

    for g in range(AHEAD):
        raw_copy(g).wait()
        start_halo(g, True)
    for g in range(AHEAD):
        start_halo(g, False)

    def near(g, carry):
        raw_copy(g).wait()
        start_halo(g, False)
        return carry

    lax.fori_loop(AHEAD, planes, near, 0)

    def levels(dark, flat):
        dark = dark.astype(jnp.float32)
        return dark, jnp.log(flat.astype(jnp.float32) - dark)

    dark_ext[pl.ds(halo, rows)], gain_ext[pl.ds(halo, rows)] = levels(dark_ref[...], flat_ref[...])
    for side in range(2):

        @pl.when(has[side])
        def _():
            for which in range(2):
                level_copy(1 - side, which).wait_recv()

        at = 0 if side == 0 else halo + rows
        dark_ext[pl.ds(at, halo)], gain_ext[pl.ds(at, halo)] = levels(
            level_ref[side, 0], level_ref[side, 1]
        )

    upper = dests // row_devices

    def target(d):
        return upper * row + d // row_devices, d % row_devices

    def is_self(d):
        a, b = target(d)
        return jnp.logical_and(a == ang, b == row)

    def is_relayed(d):
        a, b = target(d)
        return jnp.logical_and(a != ang, b // CORES != row // CORES)

    def place(a, g):
        return lines_ref.at[a * planes + g]

    def out_copy(d, g):
        a, b = target(d)
        return pltpu.make_async_remote_copy(
            src_ref=send_ref.at[d, g],
            dst_ref=place(ang, g),
            send_sem=out_send.at[d],
            recv_sem=out_recv.at[ang, g],
            device_id=(scan, a, b),
            device_id_type=MESH,
        )

    def first_hop(d, g):
        return pltpu.make_async_remote_copy(
            src_ref=send_ref.at[d, g],
            dst_ref=relay_ref.at[row, d // row_devices, g],
            send_sem=out_send.at[d],
            recv_sem=relay_recv.at[row, d // row_devices, g],
            device_id=(scan, ang, d % row_devices),
            device_id_type=MESH,
        )

    def second_hop(b, u, g):
        return pltpu.make_async_remote_copy(
            src_ref=relay_ref.at[b, u, g],
            dst_ref=place(ang, g),
            send_sem=relay_send.at[b, u],
            recv_sem=out_recv.at[ang, g],
            device_id=(scan, upper * b + u, row),
            device_id_type=MESH,
        )

    def own_copy(d, g):
        return pltpu.make_async_copy(send_ref.at[d, g], place(ang, g), out_recv.at[ang, g])

    def relays(b, u):
        return jnp.logical_and(b // CORES != row // CORES, upper * b + u != ang)

    inner = range(1, row_devices - 1)
    outer = (0, row_devices - 1)

    def relay(sources, g):
        for b in sources:
            for u in range(upper):

                @pl.when(relays(b, u))
                def _():
                    arrived = relay_ref.at[b, u, g]
                    pltpu.make_async_copy(arrived, arrived, relay_recv.at[b, u, g]).wait()
                    second_hop(b, u, g).start()

    def send(g):
        for d in range(dests):

            @pl.when(is_relayed(d))
            def _():
                first_hop(d, g).start()

        for d in range(dests):

            @pl.when(is_self(d))
            def _():
                own_copy(d, g).start()

            @pl.when(jnp.logical_not(jnp.logical_or(is_relayed(d), is_self(d))))
            def _():
                out_copy(d, g).start()

    step = cols // 2 if cols // 2 % TILE == 0 else TILE

    def lowpass(g):
        def put(at, counts, valid):
            size = counts.shape[0]
            value = gain_ext[pl.ds(at, size)] - jnp.log(
                counts.astype(jnp.float32) - dark_ext[pl.ds(at, size)]
            )
            if valid is not None:
                value = jnp.where(valid, value, 0.0)
            high, low = split(value)
            x_cat[pl.ds(at, size)] = high
            x_cat[pl.ds(ext + at, size)] = low

        put(0, halo_ref[0, g], has[0])
        put(halo, raw_ref[g], None)
        put(halo + rows, halo_ref[1, g], has[1])

        def row_pass(n, carry):
            at = pl.multiple_of(n * step, TILE)
            both = dot(row_band[...], x_cat[:, pl.ds(at, step)])
            high, low = split(both[:rows] + both[rows:])
            to = pl.multiple_of(n * step + LANES, LANES)
            z_high[:, pl.ds(to, step)] = high
            z_low[:, pl.ds(to, step)] = low
            return carry

        lax.fori_loop(0, cols // step, row_pass, 0)

        def windows(z_ref):
            return jnp.concatenate(
                [z_ref[:, n * TILE : (n + 1) * TILE + 2 * LANES] for n in range(tiles)], axis=0
            )

        both = dot(windows(z_high), col_band[...])
        rest = dot(windows(z_low), col_band[:, :TILE])
        value = both[:, :TILE] + (both[:, TILE:] + rest)
        total = jnp.zeros((rows, 1), jnp.float32)
        for n in range(tiles):
            tile = value[n * rows : (n + 1) * rows]
            low_ref[:, n * TILE : (n + 1) * TILE] = tile
            total = total + jnp.sum(tile, axis=1, keepdims=True)
        mean = total * (1.0 / cols)
        for d in range(dests):
            at = d * share
            send_ref[d, g] = (low_ref[pl.ds(at, share)] - mean[at : at + share]).astype(
                jnp.bfloat16
            )

    def build(n, carry):
        base = pl.multiple_of(n * TILE, TILE)
        strip_ref[pl.ds(base, TILE)] = ramp_block(base - (tiles - 1) * TILE)
        return carry

    def relay_inner(g, carry):
        relay(inner, g)
        return carry

    def ready(g):
        return jnp.clip(2 * (g - HOLD), 0, jnp.maximum(g, 0))

    def advance(g, carry):
        for side in range(2):

            @pl.when(has[side])
            def _():
                halo_copy(1 - side, g).wait_recv()

        lowpass(g)
        send(g)

        @pl.when(jnp.logical_and(g == 0, EXTRA > 0))
        def _():
            for more in range(EXTRA):
                start_halo(AHEAD + more, True)

        @pl.when(g + AHEAD + EXTRA < planes)
        def _():
            start_halo(g + AHEAD + EXTRA, True)

        each = -(-blocks // (planes - 1))
        lax.fori_loop(jnp.minimum(g * each, blocks), jnp.minimum((g + 1) * each, blocks), build, 0)

        @pl.when(g > 0)
        def _():
            relay(outer, g - 1)

        lax.fori_loop(ready(g - 1), ready(g), relay_inner, 0)
        return carry

    def arrive(p):
        for a in range(ang_count):
            here = place(a, p)
            pltpu.make_async_copy(here, here, out_recv.at[a, p]).wait()

    def sinogram(p, carry):
        arrive(p)
        count = ang_count * share
        for a in range(ang_count):
            line = lines_ref[a * planes + p].astype(jnp.float32)
            at = pl.ds(pl.multiple_of((a * planes + p) * share, share), share)
            for q in range(cols // LANES):
                x_ref[q, at] = line[:, q * LANES : (q + 1) * LANES]
            for k in range(tiles):
                own = k * count + a * share
                tall_ref[own : own + share] = line[:, k * TILE : (k + 1) * TILE].astype(
                    jnp.bfloat16
                )
        for shift in sorted(range(1 - tiles, tiles), key=abs):
            low, high = max(0, shift), min(tiles, tiles + shift)
            block = strip_ref[(tiles - 1 + shift) * TILE : (tiles + shift) * TILE]
            value = dot(tall_ref[low * count : high * count], block)
            here = pl.ds((low - shift) * count, (high - low) * count)
            if shift:
                acc_ref[here] += value
            else:
                acc_ref[here] = value
        for a in range(ang_count):
            for n in range(tiles):
                own = n * count + a * share
                out_stage[a * planes + p, :, n * TILE : (n + 1) * TILE] = acc_ref[
                    own : own + share
                ].astype(jnp.bfloat16)
            here = a * planes + p
            pltpu.make_async_copy(out_stage.at[here], out_ref.at[here], write_sem.at[a]).start()
        return carry

    pairs = ang_count * planes // 2
    pad = SPAN // LANES
    wide = max(planes // 3, 1)

    def gather(part):
        first, end = part * wide, (part + 1) * wide if part < 2 else planes
        pair(first, end, planes, share, partner_ref, x_ref, left_ref, right_ref)
        for r in range(share):
            product = products(r, first, end, planes, share, left_ref, right_ref)
            if part:
                product = prod_ref[r] + product
            if part < 2:
                prod_ref[r] = product
            else:
                skewed = pltpu.roll(product, 0, 1, stride=1, stride_axis=0)
                prof_ref[pl.ds(r, 1)] = jnp.sum(skewed, axis=0, keepdims=True)[:, LANES:]

    def both(g, carry):
        advance(g, carry)
        sinogram(g - BEHIND, carry)
        return carry

    lax.fori_loop(0, BEHIND, advance, 0)
    lax.fori_loop(BEHIND, planes, both, 0)
    relay(outer, planes - 1)
    lax.fori_loop(ready(planes - 1), planes, relay_inner, 0)
    for v in range(pad):
        right_ref[v] = jnp.zeros(right_ref.shape[1:], jnp.float32)
        right_ref[pad + cols // LANES + v] = jnp.zeros(right_ref.shape[1:], jnp.float32)
    if planes - BEHIND < wide + 2:
        lax.fori_loop(planes - BEHIND, wide + 2, sinogram, 0)
    gather(0)
    lax.fori_loop(max(planes - BEHIND, wide + 2), 2 * wide + 2, sinogram, 0)
    gather(1)
    lax.fori_loop(2 * wide + 2, planes, sinogram, 0)
    gather(2)
    correlate(cols, pairs, shifts_ref, corr_ref, prof_ref)

    for a in range(ang_count):
        here = pl.ds(a * planes, planes)
        pltpu.make_async_copy(out_stage.at[here], out_ref.at[here], write_sem.at[a]).wait()

    for d in range(dests):

        @pl.when(jnp.logical_not(is_self(d)))
        def _():
            sent = send_ref.at[d]
            pltpu.make_async_copy(sent, sent, out_send.at[d]).wait()

    for b in range(row_devices):
        for u in range(upper):

            @pl.when(relays(b, u))
            def _():
                sent = relay_ref.at[b, u]
                pltpu.make_async_copy(sent, sent, relay_send.at[b, u]).wait()

    for side in range(2):

        @pl.when(has[side])
        def _():
            sent = halo_ref.at[side]
            pltpu.make_async_copy(sent, sent, halo_send.at[side]).wait()

    for side in range(2):

        @pl.when(has[side])
        def _():
            for which in range(2):
                level_copy(side, which).wait_send()


def emit_kernel(sino_ref, corr_ref, sino_out, corr_out, sems):
    a = pltpu.make_async_copy(sino_ref, sino_out, sems.at[0])
    b = pltpu.make_async_copy(corr_ref, corr_out, sems.at[1])
    a.start()
    b.start()
    a.wait()
    b.wait()


def emit(sino, corr):
    hbm = pl.BlockSpec(memory_space=pl.ANY)
    return pl.pallas_call(
        emit_kernel,
        out_shape=(jax.ShapeDtypeStruct(sino.shape, sino.dtype), jax.ShapeDtypeStruct(corr.shape, corr.dtype)),
        in_specs=[hbm, hbm],
        out_specs=(hbm, hbm),
        scratch_shapes=[pltpu.SemaphoreType.DMA((2,))],
        compiler_params=pltpu.CompilerParams(vmem_limit_bytes=2**20),
    )(sino, corr)


def shards(raw_frames, dark_field, flat_field, kernel_taps, partner, shifts):
    planes, rows, cols = raw_frames.shape
    ang_count, row_devices = lax.axis_size("ang"), lax.axis_size("row")
    share = rows // ang_count
    margin = kernel_taps.shape[0] // 2
    halo = -(-margin // 16) * 16
    ext = rows + 2 * halo
    count, half = ang_count * planes, ang_count * planes // 2
    vmem = pl.BlockSpec(memory_space=pltpu.VMEM)
    hbm = pl.BlockSpec(memory_space=pl.ANY)
    bf16, f32 = jnp.bfloat16, jnp.float32
    dma = pltpu.SemaphoreType.DMA
    lines, corr = pl.pallas_call(
        functools.partial(filter_kernel, (ang_count, row_devices, halo)),
        out_shape=(
            jax.ShapeDtypeStruct((count, share, cols), bf16),
            jax.ShapeDtypeStruct((share, shifts.shape[0]), f32),
        ),
        in_specs=[pl.BlockSpec(memory_space=pltpu.HBM)] * 6,
        out_specs=(hbm, vmem),
        scratch_shapes=[
            pltpu.SMEM(kernel_taps.shape, f32),
            pltpu.SMEM(partner.shape, jnp.int32),
            pltpu.VMEM((1,) + shifts.shape, jnp.int32),
            pltpu.VMEM((planes, rows, cols), bf16),
            pltpu.VMEM((rows, cols), bf16),
            pltpu.VMEM((rows, cols), bf16),
            pltpu.VMEM((count, share, cols), bf16),
            pltpu.VMEM((2, planes, halo, cols), bf16),
            pltpu.VMEM((2, 2, halo, cols), bf16),
            pltpu.VMEM((ext, cols), f32),
            pltpu.VMEM((ext, cols), f32),
            pltpu.VMEM((2 * rows, 2 * ext), bf16),
            pltpu.VMEM((TILE + 2 * LANES, 2 * TILE), bf16),
            pltpu.VMEM((2 * ext, cols), bf16),
            pltpu.VMEM((rows, cols + 2 * LANES), bf16),
            pltpu.VMEM((rows, cols + 2 * LANES), bf16),
            pltpu.VMEM((rows, cols), f32),
            pltpu.VMEM((ang_count, planes, share, cols), bf16),
            pltpu.VMEM((row_devices, ang_count // row_devices, planes, share, cols), bf16),
            pltpu.VMEM((2 * cols - TILE, TILE), bf16),
            pltpu.VMEM((cols // LANES, count * share, LANES), f32),
            pltpu.VMEM((cols // LANES, half * share, LANES), f32),
            pltpu.VMEM(((cols + 2 * SPAN) // LANES, half * share, LANES), f32),
            pltpu.VMEM((share, LANES, 2 * SPAN + LANES), f32),
            pltpu.VMEM((share, 2 * SPAN), f32),
            pltpu.VMEM((cols // TILE * ang_count * share, TILE), bf16),
            pltpu.VMEM((cols // TILE * ang_count * share, TILE), f32),
            pltpu.VMEM((count, share, cols), bf16),
            dma((planes,)),
            dma((5,)),
            dma((ang_count,)),
            dma((2, 2)),
            dma((2, 2)),
            dma((2,)),
            dma((2, planes)),
            dma((ang_count,)),
            dma((ang_count, planes)),
            dma((row_devices, ang_count // row_devices)),
            dma((row_devices, ang_count // row_devices, planes)),
        ],
        compiler_params=pltpu.CompilerParams(collective_id=0, has_side_effects=True, vmem_limit_bytes=40 * 2**20),
    )(*(pltpu.with_memory_space_constraint(v, pltpu.HBM) for v in (kernel_taps, raw_frames, dark_field, flat_field, partner, shifts[None])))
    return emit(lines, corr)


def solution(mesh):
    in_specs = (
        P(("scan", "ang"), "row", None),
        P("row", None),
        P("row", None),
        P(),
        P("scan"),
        P(),
    )
    out_specs = (P("scan", ("ang", "row"), None), P(("scan", "ang", "row"), None))
    return jax.shard_map(shards, mesh=mesh, in_specs=in_specs, out_specs=out_specs, check_vma=False)
```

```python
import functools
import math

import jax
import jax.numpy as jnp
from jax import lax
from jax.experimental import pallas as pl
from jax.experimental.pallas import tpu as pltpu
from jax.sharding import PartitionSpec as P

SPAN = 256
LANES = 128
TILE = 256
CORES = 2
HOLD = 2
BEHIND = 5
IDLE = 2
PIECES = 1
INNER_DIRECT = 1
OUTER_DIRECT = 1
AHEAD = 2
EXTRA = 0
MESH = pl.DeviceIdType.MESH


def split(value):
    high = value.astype(jnp.bfloat16)
    low = (value - high.astype(jnp.float32)).astype(jnp.bfloat16)
    return high, low


def band(taps_ref, lag):
    tap_count = taps_ref.shape[0]
    total = jnp.zeros(lag.shape, jnp.float32)
    for tap_index in range(tap_count):
        total = jnp.where(lag == tap_index, taps_ref[tap_index], total)
    return total


def dot(left, right):
    return jnp.dot(left, right, preferred_element_type=jnp.float32)


def ramp_block(offset):
    shape = (TILE, TILE)
    distance = (
        lax.broadcasted_iota(jnp.int32, shape, 0)
        - lax.broadcasted_iota(jnp.int32, shape, 1)
        + offset
    )
    spacing = distance.astype(jnp.float32)
    odd_distance = (distance & 1) != 0
    falloff = -4.0 / (math.pi * math.pi * jnp.maximum(spacing * spacing, 1.0))
    kernel = jnp.where(distance == 0, 1.0, jnp.where(odd_distance, falloff, 0.0))
    return kernel.astype(jnp.bfloat16)


def pair(first, end, planes, share, partner_ref, x_ref, left_ref, right_ref):
    parts, count, _ = x_ref.shape
    half = count // share // 2
    pad = SPAN // LANES
    width = end - first
    base = first * (half // planes)

    def pick(k, carry):
        a, p = k // width, k % width
        i = a * planes + (first + p + 1) % planes
        offset = partner_ref[i] - i - half
        middle = half + i

        def line(index):
            return x_ref[:, pl.ds(pl.multiple_of(index * share, share), share)]

        following = line(jnp.minimum(middle + 1, 2 * half - 1))
        chosen = jnp.where(offset > 0, following, line(middle))
        place = pl.ds(pl.multiple_of((base + k) * share, share), share)
        right_ref[pl.ds(pad, parts), place] = jnp.where(offset < 0, line(middle - 1), chosen)
        left_ref[:, place] = line(i)
        return carry

    lax.fori_loop(0, (half // planes) * width, pick, 0)


def products(r, first, end, planes, share, left_ref, right_ref):
    parts, count, _ = left_ref.shape
    pairs = count // share // planes
    pad = SPAN // LANES
    rows = pl.ds(first * pairs * share + r, (end - first) * pairs, stride=share)
    left = jnp.concatenate([left_ref[q, rows] for q in range(parts)], axis=0).astype(jnp.bfloat16)
    pieces = [right_ref[v, rows] for v in range(parts + 2 * pad)]
    last = parts - 1
    right = jnp.concatenate(
        [
            jnp.concatenate([pieces[last - q + v] for q in range(parts)], axis=0)
            for v in range(2 * pad + 1)
        ],
        axis=1,
    ).astype(jnp.bfloat16)
    return lax.dot_general(
        left, right, (((0,), (0,)), ((), ())), preferred_element_type=jnp.float32
    )


def correlate(cols, half, shifts_ref, corr_ref, prof_ref):
    lane = lax.broadcasted_iota(jnp.int32, (2 * SPAN, shifts_ref.shape[1]), 0)
    selector = (SPAN - 1 - lane == shifts_ref[...]).astype(jnp.float32)
    corr_ref[...] = jnp.dot(
        prof_ref[...],
        selector,
        precision=lax.Precision.HIGHEST,
        preferred_element_type=jnp.float32,
    ) * ((half * cols) ** -0.5)


def filter_kernel(
    sizes,
    taps_hbm,
    raw_hbm,
    dark_hbm,
    flat_hbm,
    partner_hbm,
    shifts_hbm,
    out_ref,
    corr_ref,
    taps_ref,
    partner_ref,
    shifts_ref,
    raw_ref,
    dark_ref,
    flat_ref,
    lines_ref,
    halo_ref,
    level_ref,
    dark_ext,
    gain_ext,
    row_band,
    col_band,
    x_cat,
    z_high,
    z_low,
    low_ref,
    send_ref,
    relay_ref,
    strip_ref,
    x_ref,
    left_ref,
    right_ref,
    prod_ref,
    prof_ref,
    tall_ref,
    acc_ref,
    out_stage,
    raw_sem,
    field_sem,
    write_sem,
    level_send,
    level_recv,
    halo_send,
    halo_recv,
    out_send,
    out_recv,
    relay_send,
    relay_recv,
):
    ang_count, row_devices, halo = sizes
    planes, rows, cols = raw_ref.shape
    margin = taps_ref.shape[0] // 2
    dests, _, share, _ = send_ref.shape
    ext = rows + 2 * halo
    tiles = cols // TILE
    blocks = 2 * tiles - 1
    scan, ang, row = lax.axis_index("scan"), lax.axis_index("ang"), lax.axis_index("row")
    has = (row > 0, row < row_devices - 1)
    peer = (jnp.maximum(row - 1, 0), jnp.minimum(row + 1, row_devices - 1))

    def raw_copy(g):
        return pltpu.make_async_copy(raw_hbm.at[g], raw_ref.at[g], raw_sem.at[g])

    fields = (
        (taps_hbm, taps_ref),
        (dark_hbm, dark_ref),
        (flat_hbm, flat_ref),
        (partner_hbm, partner_ref),
        (shifts_hbm, shifts_ref),
    )

    def field_copy(which):
        source, target = fields[which]
        return pltpu.make_async_copy(source, target, field_sem.at[which])

    for which in range(len(fields)):
        field_copy(which).start()

    def fetch(g, carry):
        raw_copy(g).start()
        return carry

    lax.fori_loop(0, planes, fetch, 0)

    barrier = pltpu.get_barrier_semaphore()
    for a in range(ang_count):
        for b in range(row_devices):

            @pl.when(jnp.logical_or(ang != a, row != b))
            def _():
                pl.semaphore_signal(barrier, inc=1, device_id=(scan, a, b), device_id_type=MESH)

    for z_ref in (z_high, z_low):
        z_ref[:, :LANES] = jnp.zeros((rows, LANES), jnp.bfloat16)
        z_ref[:, LANES + cols :] = jnp.zeros((rows, LANES), jnp.bfloat16)

    for which in range(1, len(fields)):
        field_copy(which).wait()

    pl.semaphore_wait(barrier, ang_count * row_devices - 1)

    def level_copy(side, which):
        source = (dark_ref, flat_ref)[which]
        start = 0 if side == 0 else rows - halo
        return pltpu.make_async_remote_copy(
            src_ref=source.at[pl.ds(start, halo)],
            dst_ref=level_ref.at[1 - side, which],
            send_sem=level_send.at[side, which],
            recv_sem=level_recv.at[1 - side, which],
            device_id=(scan, ang, peer[side]),
            device_id_type=MESH,
        )

    def halo_copy(side, g):
        start = 0 if side == 0 else rows - halo
        return pltpu.make_async_remote_copy(
            src_ref=raw_ref.at[g, pl.ds(start, halo)],
            dst_ref=halo_ref.at[1 - side, g],
            send_sem=halo_send.at[side],
            recv_sem=halo_recv.at[1 - side, g],
            device_id=(scan, ang, peer[side]),
            device_id_type=MESH,
        )

    far = (row % CORES == 0, row % CORES == CORES - 1)

    def start_halo(g, distant):
        for side in range(2):

            @pl.when(jnp.logical_and(has[side], far[side] == distant))
            def _():
                halo_copy(side, g).start()

    for side in range(2):

        @pl.when(has[side])
        def _():
            for which in range(2):
                level_copy(side, which).start()

    for g in range(AHEAD):
        raw_copy(g).wait()
        start_halo(g, True)
    for g in range(AHEAD):
        start_halo(g, False)

    def near(g, carry):
        raw_copy(g).wait()
        start_halo(g, False)
        return carry

    lax.fori_loop(AHEAD, planes, near, 0)

    field_copy(0).wait()
    r_out = lax.broadcasted_iota(jnp.int32, (rows, ext), 0)
    r_in = lax.broadcasted_iota(jnp.int32, (rows, ext), 1)
    high, low = split(band(taps_ref, r_in - r_out - (halo - margin)))
    row_band[:rows, :ext] = high
    row_band[:rows, ext:] = high
    row_band[rows:, :ext] = low
    row_band[rows:, ext:] = jnp.zeros((rows, ext), jnp.bfloat16)
    c_in = lax.broadcasted_iota(jnp.int32, (TILE + 2 * LANES, TILE), 0)
    c_out = lax.broadcasted_iota(jnp.int32, (TILE + 2 * LANES, TILE), 1)
    high, low = split(band(taps_ref, c_in - c_out - (LANES - margin)))
    col_band[:, :TILE] = high
    col_band[:, TILE:] = low
    edge = jnp.logical_or(row == 0, row == row_devices - 1)

    def build(n, carry):
        base = pl.multiple_of(n * TILE, TILE)
        strip_ref[pl.ds(base, TILE)] = ramp_block(base - (tiles - 1) * TILE)
        return carry

    lax.fori_loop(0, jnp.where(edge, 0, blocks), build, 0)

    def levels(dark, flat):
        dark = dark.astype(jnp.float32)
        return dark, jnp.log(flat.astype(jnp.float32) - dark)

    dark_ext[pl.ds(halo, rows)], gain_ext[pl.ds(halo, rows)] = levels(dark_ref[...], flat_ref[...])
    for side in range(2):

        @pl.when(has[side])
        def _():
            for which in range(2):
                level_copy(1 - side, which).wait_recv()

        at = 0 if side == 0 else halo + rows
        dark_ext[pl.ds(at, halo)], gain_ext[pl.ds(at, halo)] = levels(
            level_ref[side, 0], level_ref[side, 1]
        )

    upper = dests // row_devices
    inner_hops, outer_hops = planes - INNER_DIRECT, planes - OUTER_DIRECT

    def target(d):
        return upper * row + d // row_devices, d % row_devices

    def is_self(d):
        a, b = target(d)
        return jnp.logical_and(a == ang, b == row)

    def is_relayed(d, g):
        a, b = target(d)
        crosses = jnp.logical_and(a != ang, b // CORES != row // CORES)
        return jnp.logical_and(crosses, g < jnp.where(edge, outer_hops, inner_hops))

    def place(a, g):
        return lines_ref.at[a * planes + g]

    def out_copy(d, g):
        a, b = target(d)
        return pltpu.make_async_remote_copy(
            src_ref=send_ref.at[d, g],
            dst_ref=place(ang, g),
            send_sem=out_send.at[d],
            recv_sem=out_recv.at[ang, g],
            device_id=(scan, a, b),
            device_id_type=MESH,
        )

    def first_hop(d, g):
        return pltpu.make_async_remote_copy(
            src_ref=send_ref.at[d, g],
            dst_ref=relay_ref.at[row, d // row_devices, g],
            send_sem=out_send.at[d],
            recv_sem=relay_recv.at[row, d // row_devices, g],
            device_id=(scan, ang, d % row_devices),
            device_id_type=MESH,
        )

    def second_hop(b, u, g):
        return pltpu.make_async_remote_copy(
            src_ref=relay_ref.at[b, u, g],
            dst_ref=place(ang, g),
            send_sem=relay_send.at[b, u],
            recv_sem=out_recv.at[ang, g],
            device_id=(scan, upper * b + u, row),
            device_id_type=MESH,
        )

    def own_copy(d, g):
        return pltpu.make_async_copy(send_ref.at[d, g], place(ang, g), out_recv.at[ang, g])

    def relays(b, u):
        return jnp.logical_and(b // CORES != row // CORES, upper * b + u != ang)

    inner = range(1, row_devices - 1)
    outer = (0, row_devices - 1)

    def relay(sources, g):
        for b in sources:
            for u in range(upper):

                @pl.when(relays(b, u))
                def _():
                    arrived = relay_ref.at[b, u, g]
                    pltpu.make_async_copy(arrived, arrived, relay_recv.at[b, u, g]).wait()
                    second_hop(b, u, g).start()

    def send(g):
        for d in range(dests):

            @pl.when(is_relayed(d, g))
            def _():
                first_hop(d, g).start()

        for d in range(dests):

            @pl.when(is_self(d))
            def _():
                own_copy(d, g).start()

            @pl.when(jnp.logical_not(jnp.logical_or(is_relayed(d, g), is_self(d))))
            def _():
                out_copy(d, g).start()

    step = cols // 2 if cols // 2 % TILE == 0 else TILE

    def lowpass(g):
        def put(at, counts, valid):
            size = counts.shape[0]
            value = gain_ext[pl.ds(at, size)] - jnp.log(
                counts.astype(jnp.float32) - dark_ext[pl.ds(at, size)]
            )
            if valid is not None:
                value = jnp.where(valid, value, 0.0)
            high, low = split(value)
            x_cat[pl.ds(at, size)] = high
            x_cat[pl.ds(ext + at, size)] = low

        put(0, halo_ref[0, g], has[0])
        put(halo, raw_ref[g], None)
        put(halo + rows, halo_ref[1, g], has[1])

        def row_pass(n, carry):
            at = pl.multiple_of(n * step, TILE)
            both = dot(row_band[...], x_cat[:, pl.ds(at, step)])
            high, low = split(both[:rows] + both[rows:])
            to = pl.multiple_of(n * step + LANES, LANES)
            z_high[:, pl.ds(to, step)] = high
            z_low[:, pl.ds(to, step)] = low
            return carry

        lax.fori_loop(0, cols // step, row_pass, 0)

        def windows(z_ref):
            return jnp.concatenate(
                [z_ref[:, n * TILE : (n + 1) * TILE + 2 * LANES] for n in range(tiles)], axis=0
            )

        both = dot(windows(z_high), col_band[...])
        rest = dot(windows(z_low), col_band[:, :TILE])
        value = both[:, :TILE] + (both[:, TILE:] + rest)
        total = jnp.zeros((rows, 1), jnp.float32)
        for n in range(tiles):
            tile = value[n * rows : (n + 1) * rows]
            low_ref[:, n * TILE : (n + 1) * TILE] = tile
            total = total + jnp.sum(tile, axis=1, keepdims=True)
        mean = total * (1.0 / cols)
        for d in range(dests):
            at = d * share
            send_ref[d, g] = (low_ref[pl.ds(at, share)] - mean[at : at + share]).astype(
                jnp.bfloat16
            )

    def relay_inner(g, carry):
        relay(inner, g)
        return carry

    def ready(g):
        return jnp.clip(2 * (g - HOLD), 0, jnp.clip(g, 0, inner_hops))

    def advance(g, carry):
        for side in range(2):

            @pl.when(has[side])
            def _():
                halo_copy(1 - side, g).wait_recv()

        lowpass(g)
        send(g)

        @pl.when(jnp.logical_and(g == 0, EXTRA > 0))
        def _():
            for more in range(EXTRA):
                start_halo(AHEAD + more, True)

        @pl.when(g + AHEAD + EXTRA < planes)
        def _():
            start_halo(g + AHEAD + EXTRA, True)

        each = -(-blocks // (BEHIND - IDLE))
        first = jnp.clip((g - IDLE) * each, 0, blocks)
        final = jnp.clip((g - IDLE + 1) * each, 0, blocks)
        lax.fori_loop(jnp.where(edge, first, blocks), jnp.where(edge, final, blocks), build, 0)

        @pl.when(jnp.logical_and(g > 0, g <= outer_hops))
        def _():
            relay(outer, g - 1)

        lax.fori_loop(ready(g - 1), ready(g), relay_inner, 0)
        return carry

    def arrive(p):
        for a in range(ang_count):
            here = place(a, p)
            pltpu.make_async_copy(here, here, out_recv.at[a, p]).wait()

    def sinogram(p, carry):
        arrive(p)
        count = ang_count * share
        for a in range(ang_count):
            line = lines_ref[a * planes + p].astype(jnp.float32)
            at = pl.ds(pl.multiple_of((a * planes + p) * share, share), share)
            for q in range(cols // LANES):
                x_ref[q, at] = line[:, q * LANES : (q + 1) * LANES]
            for k in range(tiles):
                own = k * count + a * share
                tall_ref[own : own + share] = line[:, k * TILE : (k + 1) * TILE].astype(
                    jnp.bfloat16
                )
        for shift in sorted(range(1 - tiles, tiles), key=abs):
            low, high = max(0, shift), min(tiles, tiles + shift)
            block = strip_ref[(tiles - 1 + shift) * TILE : (tiles + shift) * TILE]
            value = dot(tall_ref[low * count : high * count], block)
            here = pl.ds((low - shift) * count, (high - low) * count)
            if shift:
                acc_ref[here] += value
            else:
                acc_ref[here] = value
        for a in range(ang_count):
            for n in range(tiles):
                own = n * count + a * share
                out_stage[a * planes + p, :, n * TILE : (n + 1) * TILE] = acc_ref[
                    own : own + share
                ].astype(jnp.bfloat16)
            here = a * planes + p
            pltpu.make_async_copy(out_stage.at[here], out_ref.at[here], write_sem.at[a]).start()
        return carry

    pairs = ang_count * planes // 2
    pad = SPAN // LANES
    wide = max(planes // 3, 1)

    def gather(part):
        first, end = part * wide, (part + 1) * wide if part < 2 else planes
        pair(first, end, planes, share, partner_ref, x_ref, left_ref, right_ref)
        for r in range(share):
            product = products(r, first, end, planes, share, left_ref, right_ref)
            if part:
                product = prod_ref[r] + product
            if part < 2:
                prod_ref[r] = product
            else:
                skewed = pltpu.roll(product, 0, 1, stride=1, stride_axis=0)
                prof_ref[pl.ds(r, 1)] = jnp.sum(skewed, axis=0, keepdims=True)[:, LANES:]

    def both(g, carry):
        advance(g, carry)
        sinogram(g - BEHIND, carry)
        return carry

    lax.fori_loop(0, BEHIND, advance, 0)
    lax.fori_loop(BEHIND, planes, both, 0)
    if outer_hops == planes:
        relay(outer, planes - 1)
    lax.fori_loop(ready(planes - 1), inner_hops, relay_inner, 0)
    for v in range(pad):
        right_ref[v] = jnp.zeros(right_ref.shape[1:], jnp.float32)
        right_ref[pad + cols // LANES + v] = jnp.zeros(right_ref.shape[1:], jnp.float32)
    if planes - BEHIND < wide + 2:
        lax.fori_loop(planes - BEHIND, wide + 2, sinogram, 0)
    gather(0)
    lax.fori_loop(max(planes - BEHIND, wide + 2), 2 * wide + 2, sinogram, 0)
    gather(1)
    lax.fori_loop(2 * wide + 2, planes, sinogram, 0)
    gather(2)
    correlate(cols, pairs, shifts_ref, corr_ref, prof_ref)

    for a in range(ang_count):
        here = pl.ds(a * planes, planes)
        pltpu.make_async_copy(out_stage.at[here], out_ref.at[here], write_sem.at[a]).wait()

    for d in range(dests):

        @pl.when(jnp.logical_not(is_self(d)))
        def _():
            sent = send_ref.at[d]
            pltpu.make_async_copy(sent, sent, out_send.at[d]).wait()

    for b in range(row_devices):
        for u in range(upper):

            @pl.when(relays(b, u))
            def _():
                hops = inner_hops if b in inner else outer_hops
                sent = relay_ref.at[b, u, pl.ds(0, hops)]
                pltpu.make_async_copy(sent, sent, relay_send.at[b, u]).wait()

    for side in range(2):

        @pl.when(has[side])
        def _():
            sent = halo_ref.at[side]
            pltpu.make_async_copy(sent, sent, halo_send.at[side]).wait()

    for side in range(2):

        @pl.when(has[side])
        def _():
            for which in range(2):
                level_copy(side, which).wait_send()


def emit_kernel(sino_ref, corr_ref, sino_out, corr_out, sems):
    each = sino_ref.shape[0] // PIECES
    copies = [pltpu.make_async_copy(corr_ref, corr_out, sems.at[PIECES])]
    for n in range(PIECES):
        part = pl.ds(n * each, each)
        copies.append(pltpu.make_async_copy(sino_ref.at[part], sino_out.at[part], sems.at[n]))
    for copy in copies:
        copy.start()
    for copy in copies:
        copy.wait()


def emit(sino, corr):
    hbm = pl.BlockSpec(memory_space=pl.ANY)
    return pl.pallas_call(
        emit_kernel,
        out_shape=(jax.ShapeDtypeStruct(sino.shape, sino.dtype), jax.ShapeDtypeStruct(corr.shape, corr.dtype)),
        in_specs=[hbm, hbm],
        out_specs=(hbm, hbm),
        scratch_shapes=[pltpu.SemaphoreType.DMA((PIECES + 1,))],
        compiler_params=pltpu.CompilerParams(vmem_limit_bytes=2**20),
    )(sino, corr)


def shards(raw_frames, dark_field, flat_field, kernel_taps, partner, shifts):
    planes, rows, cols = raw_frames.shape
    ang_count, row_devices = lax.axis_size("ang"), lax.axis_size("row")
    share = rows // ang_count
    margin = kernel_taps.shape[0] // 2
    halo = -(-margin // 16) * 16
    ext = rows + 2 * halo
    count, half = ang_count * planes, ang_count * planes // 2
    vmem = pl.BlockSpec(memory_space=pltpu.VMEM)
    hbm = pl.BlockSpec(memory_space=pl.ANY)
    bf16, f32 = jnp.bfloat16, jnp.float32
    dma = pltpu.SemaphoreType.DMA
    lines, corr = pl.pallas_call(
        functools.partial(filter_kernel, (ang_count, row_devices, halo)),
        out_shape=(
            jax.ShapeDtypeStruct((count, share, cols), bf16),
            jax.ShapeDtypeStruct((share, shifts.shape[0]), f32),
        ),
        in_specs=[pl.BlockSpec(memory_space=pltpu.HBM)] * 6,
        out_specs=(hbm, vmem),
        scratch_shapes=[
            pltpu.SMEM(kernel_taps.shape, f32),
            pltpu.SMEM(partner.shape, jnp.int32),
            pltpu.VMEM((1,) + shifts.shape, jnp.int32),
            pltpu.VMEM((planes, rows, cols), bf16),
            pltpu.VMEM((rows, cols), bf16),
            pltpu.VMEM((rows, cols), bf16),
            pltpu.VMEM((count, share, cols), bf16),
            pltpu.VMEM((2, planes, halo, cols), bf16),
            pltpu.VMEM((2, 2, halo, cols), bf16),
            pltpu.VMEM((ext, cols), f32),
            pltpu.VMEM((ext, cols), f32),
            pltpu.VMEM((2 * rows, 2 * ext), bf16),
            pltpu.VMEM((TILE + 2 * LANES, 2 * TILE), bf16),
            pltpu.VMEM((2 * ext, cols), bf16),
            pltpu.VMEM((rows, cols + 2 * LANES), bf16),
            pltpu.VMEM((rows, cols + 2 * LANES), bf16),
            pltpu.VMEM((rows, cols), f32),
            pltpu.VMEM((ang_count, planes, share, cols), bf16),
            pltpu.VMEM((row_devices, ang_count // row_devices, planes, share, cols), bf16),
            pltpu.VMEM((2 * cols - TILE, TILE), bf16),
            pltpu.VMEM((cols // LANES, count * share, LANES), f32),
            pltpu.VMEM((cols // LANES, half * share, LANES), f32),
            pltpu.VMEM(((cols + 2 * SPAN) // LANES, half * share, LANES), f32),
            pltpu.VMEM((share, LANES, 2 * SPAN + LANES), f32),
            pltpu.VMEM((share, 2 * SPAN), f32),
            pltpu.VMEM((cols // TILE * ang_count * share, TILE), bf16),
            pltpu.VMEM((cols // TILE * ang_count * share, TILE), f32),
            pltpu.VMEM((count, share, cols), bf16),
            dma((planes,)),
            dma((5,)),
            dma((ang_count,)),
            dma((2, 2)),
            dma((2, 2)),
            dma((2,)),
            dma((2, planes)),
            dma((ang_count,)),
            dma((ang_count, planes)),
            dma((row_devices, ang_count // row_devices)),
            dma((row_devices, ang_count // row_devices, planes)),
        ],
        compiler_params=pltpu.CompilerParams(collective_id=0, has_side_effects=True, vmem_limit_bytes=40 * 2**20),
    )(*(pltpu.with_memory_space_constraint(v, pltpu.HBM) for v in (kernel_taps, raw_frames, dark_field, flat_field, partner, shifts[None])))
    return emit(lines, corr)


def solution(mesh):
    in_specs = (
        P(("scan", "ang"), "row", None),
        P("row", None),
        P("row", None),
        P(),
        P("scan"),
        P(),
    )
    out_specs = (P("scan", ("ang", "row"), None), P(("scan", "ang", "row"), None))
    return jax.shard_map(shards, mesh=mesh, in_specs=in_specs, out_specs=out_specs, check_vma=False)
```

```python
import functools
import math

import jax
import jax.numpy as jnp
from jax import lax
from jax.experimental import pallas as pl
from jax.experimental.pallas import tpu as pltpu
from jax.sharding import PartitionSpec as P

SPAN = 256
LANES = 128
TILE = 256
CORES = 2
HOLD = 2
BEHIND = 6
IDLE = 2
PIECES = 1
INNER_DIRECT = 1
OUTER_DIRECT = 1
AHEAD = 2
EXTRA = 0
MESH = pl.DeviceIdType.MESH


def split(value):
    high = value.astype(jnp.bfloat16)
    low = (value - high.astype(jnp.float32)).astype(jnp.bfloat16)
    return high, low


def band(taps_ref, lag):
    tap_count = taps_ref.shape[0]
    total = jnp.zeros(lag.shape, jnp.float32)
    for tap_index in range(tap_count):
        total = jnp.where(lag == tap_index, taps_ref[tap_index], total)
    return total


def dot(left, right):
    return jnp.dot(left, right, preferred_element_type=jnp.float32)


def ramp_block(offset):
    shape = (TILE, TILE)
    distance = (
        lax.broadcasted_iota(jnp.int32, shape, 0)
        - lax.broadcasted_iota(jnp.int32, shape, 1)
        + offset
    )
    spacing = distance.astype(jnp.float32)
    odd_distance = (distance & 1) != 0
    falloff = -4.0 / (math.pi * math.pi * jnp.maximum(spacing * spacing, 1.0))
    kernel = jnp.where(distance == 0, 1.0, jnp.where(odd_distance, falloff, 0.0))
    return kernel.astype(jnp.bfloat16)


def pair(first, end, planes, share, partner_ref, x_ref, left_ref, right_ref):
    parts, count, _ = x_ref.shape
    half = count // share // 2
    pad = SPAN // LANES
    width = end - first
    base = first * (half // planes)

    def pick(k, carry):
        a, p = k // width, k % width
        i = a * planes + (first + p + 1) % planes
        offset = partner_ref[i] - i - half
        middle = half + i

        def line(index):
            return x_ref[:, pl.ds(pl.multiple_of(index * share, share), share)]

        following = line(jnp.minimum(middle + 1, 2 * half - 1))
        chosen = jnp.where(offset > 0, following, line(middle))
        place = pl.ds(pl.multiple_of((base + k) * share, share), share)
        right_ref[pl.ds(pad, parts), place] = jnp.where(offset < 0, line(middle - 1), chosen)
        left_ref[:, place] = line(i)
        return carry

    lax.fori_loop(0, (half // planes) * width, pick, 0)


def products(r, first, end, planes, share, left_ref, right_ref):
    parts, count, _ = left_ref.shape
    pairs = count // share // planes
    pad = SPAN // LANES
    rows = pl.ds(first * pairs * share + r, (end - first) * pairs, stride=share)
    left = jnp.concatenate([left_ref[q, rows] for q in range(parts)], axis=0).astype(jnp.bfloat16)
    pieces = [right_ref[v, rows] for v in range(parts + 2 * pad)]
    last = parts - 1
    right = jnp.concatenate(
        [
            jnp.concatenate([pieces[last - q + v] for q in range(parts)], axis=0)
            for v in range(2 * pad + 1)
        ],
        axis=1,
    ).astype(jnp.bfloat16)
    return lax.dot_general(
        left, right, (((0,), (0,)), ((), ())), preferred_element_type=jnp.float32
    )


def correlate(cols, half, shifts_ref, corr_ref, prof_ref):
    lane = lax.broadcasted_iota(jnp.int32, (2 * SPAN, shifts_ref.shape[1]), 0)
    selector = (SPAN - 1 - lane == shifts_ref[...]).astype(jnp.float32)
    corr_ref[...] = jnp.dot(
        prof_ref[...],
        selector,
        precision=lax.Precision.HIGHEST,
        preferred_element_type=jnp.float32,
    ) * ((half * cols) ** -0.5)


def filter_kernel(
    sizes,
    taps_hbm,
    raw_hbm,
    dark_hbm,
    flat_hbm,
    partner_hbm,
    shifts_hbm,
    out_ref,
    corr_ref,
    taps_ref,
    partner_ref,
    shifts_ref,
    raw_ref,
    dark_ref,
    flat_ref,
    lines_ref,
    halo_ref,
    level_ref,
    dark_ext,
    gain_ext,
    row_band,
    col_band,
    x_cat,
    z_high,
    z_low,
    low_ref,
    send_ref,
    relay_ref,
    strip_ref,
    x_ref,
    left_ref,
    right_ref,
    prod_ref,
    prof_ref,
    tall_ref,
    acc_ref,
    out_stage,
    raw_sem,
    field_sem,
    write_sem,
    level_send,
    level_recv,
    halo_send,
    halo_recv,
    out_send,
    out_recv,
    relay_send,
    relay_recv,
):
    ang_count, row_devices, halo = sizes
    planes, rows, cols = raw_ref.shape
    margin = taps_ref.shape[0] // 2
    dests, _, share, _ = send_ref.shape
    ext = rows + 2 * halo
    tiles = cols // TILE
    blocks = 2 * tiles - 1
    scan, ang, row = lax.axis_index("scan"), lax.axis_index("ang"), lax.axis_index("row")
    has = (row > 0, row < row_devices - 1)
    peer = (jnp.maximum(row - 1, 0), jnp.minimum(row + 1, row_devices - 1))

    def raw_copy(g):
        return pltpu.make_async_copy(raw_hbm.at[g], raw_ref.at[g], raw_sem.at[g])

    fields = (
        (taps_hbm, taps_ref),
        (dark_hbm, dark_ref),
        (flat_hbm, flat_ref),
        (partner_hbm, partner_ref),
        (shifts_hbm, shifts_ref),
    )

    def field_copy(which):
        source, target = fields[which]
        return pltpu.make_async_copy(source, target, field_sem.at[which])

    for which in range(len(fields)):
        field_copy(which).start()

    def fetch(g, carry):
        raw_copy(g).start()
        return carry

    lax.fori_loop(0, planes, fetch, 0)

    barrier = pltpu.get_barrier_semaphore()
    for a in range(ang_count):
        for b in range(row_devices):

            @pl.when(jnp.logical_or(ang != a, row != b))
            def _():
                pl.semaphore_signal(barrier, inc=1, device_id=(scan, a, b), device_id_type=MESH)

    for z_ref in (z_high, z_low):
        z_ref[:, :LANES] = jnp.zeros((rows, LANES), jnp.bfloat16)
        z_ref[:, LANES + cols :] = jnp.zeros((rows, LANES), jnp.bfloat16)

    for which in range(1, len(fields)):
        field_copy(which).wait()

    pl.semaphore_wait(barrier, ang_count * row_devices - 1)

    def level_copy(side, which):
        source = (dark_ref, flat_ref)[which]
        start = 0 if side == 0 else rows - halo
        return pltpu.make_async_remote_copy(
            src_ref=source.at[pl.ds(start, halo)],
            dst_ref=level_ref.at[1 - side, which],
            send_sem=level_send.at[side, which],
            recv_sem=level_recv.at[1 - side, which],
            device_id=(scan, ang, peer[side]),
            device_id_type=MESH,
        )

    def halo_copy(side, g):
        start = 0 if side == 0 else rows - halo
        return pltpu.make_async_remote_copy(
            src_ref=raw_ref.at[g, pl.ds(start, halo)],
            dst_ref=halo_ref.at[1 - side, g],
            send_sem=halo_send.at[side],
            recv_sem=halo_recv.at[1 - side, g],
            device_id=(scan, ang, peer[side]),
            device_id_type=MESH,
        )

    far = (row % CORES == 0, row % CORES == CORES - 1)

    def start_halo(g, distant):
        for side in range(2):

            @pl.when(jnp.logical_and(has[side], far[side] == distant))
            def _():
                halo_copy(side, g).start()

    for side in range(2):

        @pl.when(has[side])
        def _():
            for which in range(2):
                level_copy(side, which).start()

    for g in range(AHEAD):
        raw_copy(g).wait()
        start_halo(g, True)
    for g in range(AHEAD):
        start_halo(g, False)

    def near(g, carry):
        raw_copy(g).wait()
        start_halo(g, False)
        return carry

    lax.fori_loop(AHEAD, planes, near, 0)

    field_copy(0).wait()
    r_out = lax.broadcasted_iota(jnp.int32, (rows, ext), 0)
    r_in = lax.broadcasted_iota(jnp.int32, (rows, ext), 1)
    high, low = split(band(taps_ref, r_in - r_out - (halo - margin)))
    row_band[:rows, :ext] = high
    row_band[:rows, ext:] = high
    row_band[rows:, :ext] = low
    row_band[rows:, ext:] = jnp.zeros((rows, ext), jnp.bfloat16)
    c_in = lax.broadcasted_iota(jnp.int32, (TILE + 2 * LANES, TILE), 0)
    c_out = lax.broadcasted_iota(jnp.int32, (TILE + 2 * LANES, TILE), 1)
    high, low = split(band(taps_ref, c_in - c_out - (LANES - margin)))
    col_band[:, :TILE] = high
    col_band[:, TILE:] = low
    edge = jnp.logical_or(row == 0, row == row_devices - 1)

    def build(n, carry):
        base = pl.multiple_of(n * TILE, TILE)
        strip_ref[pl.ds(base, TILE)] = ramp_block(base - (tiles - 1) * TILE)
        return carry

    lax.fori_loop(0, jnp.where(edge, 0, blocks), build, 0)

    def levels(dark, flat):
        dark = dark.astype(jnp.float32)
        return dark, jnp.log(flat.astype(jnp.float32) - dark)

    dark_ext[pl.ds(halo, rows)], gain_ext[pl.ds(halo, rows)] = levels(dark_ref[...], flat_ref[...])
    for side in range(2):

        @pl.when(has[side])
        def _():
            for which in range(2):
                level_copy(1 - side, which).wait_recv()

        at = 0 if side == 0 else halo + rows
        dark_ext[pl.ds(at, halo)], gain_ext[pl.ds(at, halo)] = levels(
            level_ref[side, 0], level_ref[side, 1]
        )

    upper = dests // row_devices
    inner_hops, outer_hops = planes - INNER_DIRECT, planes - OUTER_DIRECT

    def target(d):
        return upper * row + d // row_devices, d % row_devices

    def is_self(d):
        a, b = target(d)
        return jnp.logical_and(a == ang, b == row)

    def is_relayed(d, g):
        a, b = target(d)
        crosses = jnp.logical_and(a != ang, b // CORES != row // CORES)
        return jnp.logical_and(crosses, g < jnp.where(edge, outer_hops, inner_hops))

    def place(a, g):
        return lines_ref.at[a * planes + g]

    def out_copy(d, g):
        a, b = target(d)
        return pltpu.make_async_remote_copy(
            src_ref=send_ref.at[d, g],
            dst_ref=place(ang, g),
            send_sem=out_send.at[d],
            recv_sem=out_recv.at[ang, g],
            device_id=(scan, a, b),
            device_id_type=MESH,
        )

    def first_hop(d, g):
        return pltpu.make_async_remote_copy(
            src_ref=send_ref.at[d, g],
            dst_ref=relay_ref.at[row, d // row_devices, g],
            send_sem=out_send.at[d],
            recv_sem=relay_recv.at[row, d // row_devices, g],
            device_id=(scan, ang, d % row_devices),
            device_id_type=MESH,
        )

    def second_hop(b, u, g):
        return pltpu.make_async_remote_copy(
            src_ref=relay_ref.at[b, u, g],
            dst_ref=place(ang, g),
            send_sem=relay_send.at[b, u],
            recv_sem=out_recv.at[ang, g],
            device_id=(scan, upper * b + u, row),
            device_id_type=MESH,
        )

    def own_copy(d, g):
        return pltpu.make_async_copy(send_ref.at[d, g], place(ang, g), out_recv.at[ang, g])

    def relays(b, u):
        return jnp.logical_and(b // CORES != row // CORES, upper * b + u != ang)

    inner = range(1, row_devices - 1)
    outer = (0, row_devices - 1)

    def relay(sources, g):
        for b in sources:
            for u in range(upper):

                @pl.when(relays(b, u))
                def _():
                    arrived = relay_ref.at[b, u, g]
                    pltpu.make_async_copy(arrived, arrived, relay_recv.at[b, u, g]).wait()
                    second_hop(b, u, g).start()

    def send(g):
        for d in range(dests):

            @pl.when(is_relayed(d, g))
            def _():
                first_hop(d, g).start()

        for d in range(dests):

            @pl.when(is_self(d))
            def _():
                own_copy(d, g).start()

            @pl.when(jnp.logical_not(jnp.logical_or(is_relayed(d, g), is_self(d))))
            def _():
                out_copy(d, g).start()

    step = cols // 2 if cols // 2 % TILE == 0 else TILE

    def lowpass(g):
        def put(at, counts, valid):
            size = counts.shape[0]
            value = gain_ext[pl.ds(at, size)] - jnp.log(
                counts.astype(jnp.float32) - dark_ext[pl.ds(at, size)]
            )
            if valid is not None:
                value = jnp.where(valid, value, 0.0)
            high, low = split(value)
            x_cat[pl.ds(at, size)] = high
            x_cat[pl.ds(ext + at, size)] = low

        put(0, halo_ref[0, g], has[0])
        put(halo, raw_ref[g], None)
        put(halo + rows, halo_ref[1, g], has[1])

        def row_pass(n, carry):
            at = pl.multiple_of(n * step, TILE)
            both = dot(row_band[...], x_cat[:, pl.ds(at, step)])
            high, low = split(both[:rows] + both[rows:])
            to = pl.multiple_of(n * step + LANES, LANES)
            z_high[:, pl.ds(to, step)] = high
            z_low[:, pl.ds(to, step)] = low
            return carry

        lax.fori_loop(0, cols // step, row_pass, 0)

        def windows(z_ref):
            return jnp.concatenate(
                [z_ref[:, n * TILE : (n + 1) * TILE + 2 * LANES] for n in range(tiles)], axis=0
            )

        both = dot(windows(z_high), col_band[...])
        rest = dot(windows(z_low), col_band[:, :TILE])
        value = both[:, :TILE] + (both[:, TILE:] + rest)
        total = jnp.zeros((rows, 1), jnp.float32)
        for n in range(tiles):
            tile = value[n * rows : (n + 1) * rows]
            low_ref[:, n * TILE : (n + 1) * TILE] = tile
            total = total + jnp.sum(tile, axis=1, keepdims=True)
        mean = total * (1.0 / cols)
        for d in range(dests):
            at = d * share
            send_ref[d, g] = (low_ref[pl.ds(at, share)] - mean[at : at + share]).astype(
                jnp.bfloat16
            )

    def relay_inner(g, carry):
        relay(inner, g)
        return carry

    def ready(g):
        return jnp.clip(2 * (g - HOLD), 0, jnp.clip(g, 0, inner_hops))

    def advance(g, carry):
        for side in range(2):

            @pl.when(has[side])
            def _():
                halo_copy(1 - side, g).wait_recv()

        lowpass(g)
        send(g)

        @pl.when(jnp.logical_and(g == 0, EXTRA > 0))
        def _():
            for more in range(EXTRA):
                start_halo(AHEAD + more, True)

        @pl.when(g + AHEAD + EXTRA < planes)
        def _():
            start_halo(g + AHEAD + EXTRA, True)

        each = -(-blocks // (BEHIND - IDLE))
        first = jnp.clip((g - IDLE) * each, 0, blocks)
        final = jnp.clip((g - IDLE + 1) * each, 0, blocks)
        lax.fori_loop(jnp.where(edge, first, blocks), jnp.where(edge, final, blocks), build, 0)

        return carry

    def forward(g, carry):
        @pl.when(jnp.logical_and(g > 0, g <= outer_hops))
        def _():
            relay(outer, g - 1)

        lax.fori_loop(ready(g - 1), ready(g), relay_inner, 0)
        return carry

    def arrive(p):
        for a in range(ang_count):
            here = place(a, p)
            pltpu.make_async_copy(here, here, out_recv.at[a, p]).wait()

    def sinogram(p, carry):
        arrive(p)
        count = ang_count * share
        for a in range(ang_count):
            line = lines_ref[a * planes + p].astype(jnp.float32)
            at = pl.ds(pl.multiple_of((a * planes + p) * share, share), share)
            for q in range(cols // LANES):
                x_ref[q, at] = line[:, q * LANES : (q + 1) * LANES]
            for k in range(tiles):
                own = k * count + a * share
                tall_ref[own : own + share] = line[:, k * TILE : (k + 1) * TILE].astype(
                    jnp.bfloat16
                )
        for shift in sorted(range(1 - tiles, tiles), key=abs):
            low, high = max(0, shift), min(tiles, tiles + shift)
            block = strip_ref[(tiles - 1 + shift) * TILE : (tiles + shift) * TILE]
            value = dot(tall_ref[low * count : high * count], block)
            here = pl.ds((low - shift) * count, (high - low) * count)
            if shift:
                acc_ref[here] += value
            else:
                acc_ref[here] = value
        for a in range(ang_count):
            for n in range(tiles):
                own = n * count + a * share
                out_stage[a * planes + p, :, n * TILE : (n + 1) * TILE] = acc_ref[
                    own : own + share
                ].astype(jnp.bfloat16)
            here = a * planes + p
            pltpu.make_async_copy(out_stage.at[here], out_ref.at[here], write_sem.at[a]).start()
        return carry

    pairs = ang_count * planes // 2
    pad = SPAN // LANES
    wide = max(planes // 3, 1)

    def gather(part):
        first, end = part * wide, (part + 1) * wide if part < 2 else planes
        pair(first, end, planes, share, partner_ref, x_ref, left_ref, right_ref)
        for r in range(share):
            product = products(r, first, end, planes, share, left_ref, right_ref)
            if part == 1:
                product = prod_ref[r] + product
            if part:
                skewed = pltpu.roll(product, 0, 1, stride=1, stride_axis=0)
                line = jnp.sum(skewed, axis=0, keepdims=True)[:, LANES:]
                prof_ref[pl.ds(r, 1)] = line if part == 1 else prof_ref[pl.ds(r, 1)] + line
            else:
                prod_ref[r] = product

    def both(g, carry):
        advance(g, carry)
        sinogram(g - BEHIND, carry)
        return forward(g, carry)

    def first(g, carry):
        advance(g, carry)
        return forward(g, carry)

    lax.fori_loop(0, BEHIND, first, 0)
    lax.fori_loop(BEHIND, planes, both, 0)
    if outer_hops == planes:
        relay(outer, planes - 1)
    lax.fori_loop(ready(planes - 1), inner_hops, relay_inner, 0)
    for v in range(pad):
        right_ref[v] = jnp.zeros(right_ref.shape[1:], jnp.float32)
        right_ref[pad + cols // LANES + v] = jnp.zeros(right_ref.shape[1:], jnp.float32)
    if planes - BEHIND < wide + 2:
        lax.fori_loop(planes - BEHIND, wide + 2, sinogram, 0)
    gather(0)
    lax.fori_loop(max(planes - BEHIND, wide + 2), 2 * wide + 2, sinogram, 0)
    gather(1)
    lax.fori_loop(2 * wide + 2, planes, sinogram, 0)
    gather(2)
    correlate(cols, pairs, shifts_ref, corr_ref, prof_ref)

    for a in range(ang_count):
        here = pl.ds(a * planes, planes)
        pltpu.make_async_copy(out_stage.at[here], out_ref.at[here], write_sem.at[a]).wait()

    for d in range(dests):

        @pl.when(jnp.logical_not(is_self(d)))
        def _():
            sent = send_ref.at[d]
            pltpu.make_async_copy(sent, sent, out_send.at[d]).wait()

    for b in range(row_devices):
        for u in range(upper):

            @pl.when(relays(b, u))
            def _():
                hops = inner_hops if b in inner else outer_hops
                sent = relay_ref.at[b, u, pl.ds(0, hops)]
                pltpu.make_async_copy(sent, sent, relay_send.at[b, u]).wait()

    for side in range(2):

        @pl.when(has[side])
        def _():
            sent = halo_ref.at[side]
            pltpu.make_async_copy(sent, sent, halo_send.at[side]).wait()

    for side in range(2):

        @pl.when(has[side])
        def _():
            for which in range(2):
                level_copy(side, which).wait_send()


def emit_kernel(sino_ref, corr_ref, sino_out, corr_out, sems):
    each = sino_ref.shape[0] // PIECES
    copies = [pltpu.make_async_copy(corr_ref, corr_out, sems.at[PIECES])]
    for n in range(PIECES):
        part = pl.ds(n * each, each)
        copies.append(pltpu.make_async_copy(sino_ref.at[part], sino_out.at[part], sems.at[n]))
    for copy in copies:
        copy.start()
    for copy in copies:
        copy.wait()


def emit(sino, corr):
    hbm = pl.BlockSpec(memory_space=pl.ANY)
    return pl.pallas_call(
        emit_kernel,
        out_shape=(jax.ShapeDtypeStruct(sino.shape, sino.dtype), jax.ShapeDtypeStruct(corr.shape, corr.dtype)),
        in_specs=[hbm, hbm],
        out_specs=(hbm, hbm),
        scratch_shapes=[pltpu.SemaphoreType.DMA((PIECES + 1,))],
        compiler_params=pltpu.CompilerParams(vmem_limit_bytes=2**20),
    )(sino, corr)


def shards(raw_frames, dark_field, flat_field, kernel_taps, partner, shifts):
    planes, rows, cols = raw_frames.shape
    ang_count, row_devices = lax.axis_size("ang"), lax.axis_size("row")
    share = rows // ang_count
    margin = kernel_taps.shape[0] // 2
    halo = -(-margin // 16) * 16
    ext = rows + 2 * halo
    count, half = ang_count * planes, ang_count * planes // 2
    vmem = pl.BlockSpec(memory_space=pltpu.VMEM)
    hbm = pl.BlockSpec(memory_space=pl.ANY)
    bf16, f32 = jnp.bfloat16, jnp.float32
    dma = pltpu.SemaphoreType.DMA
    lines, corr = pl.pallas_call(
        functools.partial(filter_kernel, (ang_count, row_devices, halo)),
        out_shape=(
            jax.ShapeDtypeStruct((count, share, cols), bf16),
            jax.ShapeDtypeStruct((share, shifts.shape[0]), f32),
        ),
        in_specs=[pl.BlockSpec(memory_space=pltpu.HBM)] * 6,
        out_specs=(hbm, vmem),
        scratch_shapes=[
            pltpu.SMEM(kernel_taps.shape, f32),
            pltpu.SMEM(partner.shape, jnp.int32),
            pltpu.VMEM((1,) + shifts.shape, jnp.int32),
            pltpu.VMEM((planes, rows, cols), bf16),
            pltpu.VMEM((rows, cols), bf16),
            pltpu.VMEM((rows, cols), bf16),
            pltpu.VMEM((count, share, cols), bf16),
            pltpu.VMEM((2, planes, halo, cols), bf16),
            pltpu.VMEM((2, 2, halo, cols), bf16),
            pltpu.VMEM((ext, cols), f32),
            pltpu.VMEM((ext, cols), f32),
            pltpu.VMEM((2 * rows, 2 * ext), bf16),
            pltpu.VMEM((TILE + 2 * LANES, 2 * TILE), bf16),
            pltpu.VMEM((2 * ext, cols), bf16),
            pltpu.VMEM((rows, cols + 2 * LANES), bf16),
            pltpu.VMEM((rows, cols + 2 * LANES), bf16),
            pltpu.VMEM((rows, cols), f32),
            pltpu.VMEM((ang_count, planes, share, cols), bf16),
            pltpu.VMEM((row_devices, ang_count // row_devices, planes, share, cols), bf16),
            pltpu.VMEM((2 * cols - TILE, TILE), bf16),
            pltpu.VMEM((cols // LANES, count * share, LANES), f32),
            pltpu.VMEM((cols // LANES, half * share, LANES), f32),
            pltpu.VMEM(((cols + 2 * SPAN) // LANES, half * share, LANES), f32),
            pltpu.VMEM((share, LANES, 2 * SPAN + LANES), f32),
            pltpu.VMEM((share, 2 * SPAN), f32),
            pltpu.VMEM((cols // TILE * ang_count * share, TILE), bf16),
            pltpu.VMEM((cols // TILE * ang_count * share, TILE), f32),
            pltpu.VMEM((count, share, cols), bf16),
            dma((planes,)),
            dma((5,)),
            dma((ang_count,)),
            dma((2, 2)),
            dma((2, 2)),
            dma((2,)),
            dma((2, planes)),
            dma((ang_count,)),
            dma((ang_count, planes)),
            dma((row_devices, ang_count // row_devices)),
            dma((row_devices, ang_count // row_devices, planes)),
        ],
        compiler_params=pltpu.CompilerParams(collective_id=0, has_side_effects=True, vmem_limit_bytes=40 * 2**20),
    )(*(pltpu.with_memory_space_constraint(v, pltpu.HBM) for v in (kernel_taps, raw_frames, dark_field, flat_field, partner, shifts[None])))
    return emit(lines, corr)


def solution(mesh):
    in_specs = (
        P(("scan", "ang"), "row", None),
        P("row", None),
        P("row", None),
        P(),
        P("scan"),
        P(),
    )
    out_specs = (P("scan", ("ang", "row"), None), P(("scan", "ang", "row"), None))
    return jax.shard_map(shards, mesh=mesh, in_specs=in_specs, out_specs=out_specs, check_vma=False)
```

```python
import functools
import math

import jax
import jax.numpy as jnp
from jax import lax
from jax.experimental import pallas as pl
from jax.experimental.pallas import tpu as pltpu
from jax.sharding import PartitionSpec as P

SPAN = 256
LANES = 128
TILE = 256
CORES = 2
HOLD = 2
BEHIND = 5
IDLE = 1
PIECES = 1
INNER_DIRECT = 1
OUTER_DIRECT = 1
AHEAD = 2
EXTRA = 0
MESH = pl.DeviceIdType.MESH


def split(value):
    high = value.astype(jnp.bfloat16)
    low = (value - high.astype(jnp.float32)).astype(jnp.bfloat16)
    return high, low


def band(taps_ref, lag):
    tap_count = taps_ref.shape[0]
    total = jnp.zeros(lag.shape, jnp.float32)
    for tap_index in range(tap_count):
        total = jnp.where(lag == tap_index, taps_ref[tap_index], total)
    return total


def dot(left, right):
    return jnp.dot(left, right, preferred_element_type=jnp.float32)


def ramp_block(offset):
    shape = (TILE, TILE)
    distance = (
        lax.broadcasted_iota(jnp.int32, shape, 0)
        - lax.broadcasted_iota(jnp.int32, shape, 1)
        + offset
    )
    spacing = distance.astype(jnp.float32)
    odd_distance = (distance & 1) != 0
    falloff = -4.0 / (math.pi * math.pi * jnp.maximum(spacing * spacing, 1.0))
    kernel = jnp.where(distance == 0, 1.0, jnp.where(odd_distance, falloff, 0.0))
    return kernel.astype(jnp.bfloat16)


def pair(first, end, planes, share, partner_ref, x_ref, left_ref, right_ref):
    parts, count, _ = x_ref.shape
    half = count // share // 2
    pad = SPAN // LANES
    width = end - first
    base = first * (half // planes)

    def pick(k, carry):
        a, p = k // width, k % width
        i = a * planes + (first + p + 1) % planes
        offset = partner_ref[i] - i - half
        middle = half + i

        def line(index):
            return x_ref[:, pl.ds(pl.multiple_of(index * share, share), share)]

        following = line(jnp.minimum(middle + 1, 2 * half - 1))
        chosen = jnp.where(offset > 0, following, line(middle))
        place = pl.ds(pl.multiple_of((base + k) * share, share), share)
        right_ref[pl.ds(pad, parts), place] = jnp.where(offset < 0, line(middle - 1), chosen)
        left_ref[:, place] = line(i)
        return carry

    lax.fori_loop(0, (half // planes) * width, pick, 0)


def products(r, first, end, planes, share, left_ref, right_ref):
    parts, count, _ = left_ref.shape
    pairs = count // share // planes
    pad = SPAN // LANES
    rows = pl.ds(first * pairs * share + r, (end - first) * pairs, stride=share)
    left = jnp.concatenate([left_ref[q, rows] for q in range(parts)], axis=0).astype(jnp.bfloat16)
    pieces = [right_ref[v, rows] for v in range(parts + 2 * pad)]
    last = parts - 1
    right = jnp.concatenate(
        [
            jnp.concatenate([pieces[last - q + v] for q in range(parts)], axis=0)
            for v in range(2 * pad + 1)
        ],
        axis=1,
    ).astype(jnp.bfloat16)
    return lax.dot_general(
        left, right, (((0,), (0,)), ((), ())), preferred_element_type=jnp.float32
    )


def correlate(cols, half, shifts_ref, corr_ref, prof_ref):
    lane = lax.broadcasted_iota(jnp.int32, (2 * SPAN, shifts_ref.shape[1]), 0)
    selector = (SPAN - 1 - lane == shifts_ref[...]).astype(jnp.float32)
    corr_ref[...] = jnp.dot(
        prof_ref[...],
        selector,
        precision=lax.Precision.HIGHEST,
        preferred_element_type=jnp.float32,
    ) * ((half * cols) ** -0.5)


def filter_kernel(
    sizes,
    taps_hbm,
    raw_hbm,
    dark_hbm,
    flat_hbm,
    partner_hbm,
    shifts_hbm,
    out_ref,
    corr_ref,
    taps_ref,
    partner_ref,
    shifts_ref,
    raw_ref,
    dark_ref,
    flat_ref,
    lines_ref,
    halo_ref,
    level_ref,
    dark_ext,
    gain_ext,
    row_band,
    col_band,
    x_cat,
    z_high,
    z_low,
    low_ref,
    send_ref,
    relay_ref,
    strip_ref,
    x_ref,
    left_ref,
    right_ref,
    prod_ref,
    prof_ref,
    tall_ref,
    acc_ref,
    out_stage,
    raw_sem,
    field_sem,
    write_sem,
    level_send,
    level_recv,
    halo_send,
    halo_recv,
    out_send,
    out_recv,
    relay_send,
    relay_recv,
):
    ang_count, row_devices, halo = sizes
    planes, rows, cols = raw_ref.shape
    margin = taps_ref.shape[0] // 2
    dests, _, share, _ = send_ref.shape
    ext = rows + 2 * halo
    tiles = cols // TILE
    blocks = 2 * tiles - 1
    scan, ang, row = lax.axis_index("scan"), lax.axis_index("ang"), lax.axis_index("row")
    has = (row > 0, row < row_devices - 1)
    peer = (jnp.maximum(row - 1, 0), jnp.minimum(row + 1, row_devices - 1))

    def raw_copy(g):
        return pltpu.make_async_copy(raw_hbm.at[g], raw_ref.at[g], raw_sem.at[g])

    fields = (
        (taps_hbm, taps_ref),
        (dark_hbm, dark_ref),
        (flat_hbm, flat_ref),
        (partner_hbm, partner_ref),
        (shifts_hbm, shifts_ref),
    )

    def field_copy(which):
        source, target = fields[which]
        return pltpu.make_async_copy(source, target, field_sem.at[which])

    for which in range(len(fields)):
        field_copy(which).start()

    def fetch(g, carry):
        raw_copy(g).start()
        return carry

    lax.fori_loop(0, planes, fetch, 0)

    barrier = pltpu.get_barrier_semaphore()
    for a in range(ang_count):
        for b in range(row_devices):

            @pl.when(jnp.logical_or(ang != a, row != b))
            def _():
                pl.semaphore_signal(barrier, inc=1, device_id=(scan, a, b), device_id_type=MESH)

    for z_ref in (z_high, z_low):
        z_ref[:, :LANES] = jnp.zeros((rows, LANES), jnp.bfloat16)
        z_ref[:, LANES + cols :] = jnp.zeros((rows, LANES), jnp.bfloat16)

    for which in range(1, len(fields)):
        field_copy(which).wait()

    pl.semaphore_wait(barrier, ang_count * row_devices - 1)

    def level_copy(side, which):
        source = (dark_ref, flat_ref)[which]
        start = 0 if side == 0 else rows - halo
        return pltpu.make_async_remote_copy(
            src_ref=source.at[pl.ds(start, halo)],
            dst_ref=level_ref.at[1 - side, which],
            send_sem=level_send.at[side, which],
            recv_sem=level_recv.at[1 - side, which],
            device_id=(scan, ang, peer[side]),
            device_id_type=MESH,
        )

    def halo_copy(side, g):
        start = 0 if side == 0 else rows - halo
        return pltpu.make_async_remote_copy(
            src_ref=raw_ref.at[g, pl.ds(start, halo)],
            dst_ref=halo_ref.at[1 - side, g],
            send_sem=halo_send.at[side],
            recv_sem=halo_recv.at[1 - side, g],
            device_id=(scan, ang, peer[side]),
            device_id_type=MESH,
        )

    far = (row % CORES == 0, row % CORES == CORES - 1)

    def start_halo(g, distant):
        for side in range(2):

            @pl.when(jnp.logical_and(has[side], far[side] == distant))
            def _():
                halo_copy(side, g).start()

    for side in range(2):

        @pl.when(has[side])
        def _():
            for which in range(2):
                level_copy(side, which).start()

    for g in range(AHEAD):
        raw_copy(g).wait()
        start_halo(g, True)
    for g in range(AHEAD):
        start_halo(g, False)

    def near(g, carry):
        raw_copy(g).wait()
        start_halo(g, False)
        return carry

    lax.fori_loop(AHEAD, planes, near, 0)

    field_copy(0).wait()
    r_out = lax.broadcasted_iota(jnp.int32, (rows, ext), 0)
    r_in = lax.broadcasted_iota(jnp.int32, (rows, ext), 1)
    high, low = split(band(taps_ref, r_in - r_out - (halo - margin)))
    row_band[:rows, :ext] = high
    row_band[:rows, ext:] = high
    row_band[rows:, :ext] = low
    row_band[rows:, ext:] = jnp.zeros((rows, ext), jnp.bfloat16)
    c_in = lax.broadcasted_iota(jnp.int32, (TILE + 2 * LANES, TILE), 0)
    c_out = lax.broadcasted_iota(jnp.int32, (TILE + 2 * LANES, TILE), 1)
    high, low = split(band(taps_ref, c_in - c_out - (LANES - margin)))
    col_band[:, :TILE] = high
    col_band[:, TILE:] = low
    edge = jnp.logical_or(row == 0, row == row_devices - 1)

    def build(n, carry):
        base = pl.multiple_of(n * TILE, TILE)
        strip_ref[pl.ds(base, TILE)] = ramp_block(base - (tiles - 1) * TILE)
        return carry

    lax.fori_loop(0, jnp.where(edge, 0, blocks), build, 0)

    def levels(dark, flat):
        dark = dark.astype(jnp.float32)
        return dark, jnp.log(flat.astype(jnp.float32) - dark)

    dark_ext[pl.ds(halo, rows)], gain_ext[pl.ds(halo, rows)] = levels(dark_ref[...], flat_ref[...])
    for side in range(2):

        @pl.when(has[side])
        def _():
            for which in range(2):
                level_copy(1 - side, which).wait_recv()

        at = 0 if side == 0 else halo + rows
        dark_ext[pl.ds(at, halo)], gain_ext[pl.ds(at, halo)] = levels(
            level_ref[side, 0], level_ref[side, 1]
        )

    upper = dests // row_devices
    inner_hops, outer_hops = planes - INNER_DIRECT, planes - OUTER_DIRECT

    def target(d):
        return upper * row + d // row_devices, d % row_devices

    def is_self(d):
        a, b = target(d)
        return jnp.logical_and(a == ang, b == row)

    def is_relayed(d, g):
        a, b = target(d)
        crosses = jnp.logical_and(a != ang, b // CORES != row // CORES)
        return jnp.logical_and(crosses, g < jnp.where(edge, outer_hops, inner_hops))

    def place(a, g):
        return lines_ref.at[a * planes + g]

    def out_copy(d, g):
        a, b = target(d)
        return pltpu.make_async_remote_copy(
            src_ref=send_ref.at[d, g],
            dst_ref=place(ang, g),
            send_sem=out_send.at[d],
            recv_sem=out_recv.at[ang, g],
            device_id=(scan, a, b),
            device_id_type=MESH,
        )

    def first_hop(d, g):
        return pltpu.make_async_remote_copy(
            src_ref=send_ref.at[d, g],
            dst_ref=relay_ref.at[row, d // row_devices, g],
            send_sem=out_send.at[d],
            recv_sem=relay_recv.at[row, d // row_devices, g],
            device_id=(scan, ang, d % row_devices),
            device_id_type=MESH,
        )

    def second_hop(b, u, g):
        return pltpu.make_async_remote_copy(
            src_ref=relay_ref.at[b, u, g],
            dst_ref=place(ang, g),
            send_sem=relay_send.at[b, u],
            recv_sem=out_recv.at[ang, g],
            device_id=(scan, upper * b + u, row),
            device_id_type=MESH,
        )

    def own_copy(d, g):
        return pltpu.make_async_copy(send_ref.at[d, g], place(ang, g), out_recv.at[ang, g])

    def relays(b, u):
        return jnp.logical_and(b // CORES != row // CORES, upper * b + u != ang)

    inner = range(1, row_devices - 1)
    outer = (0, row_devices - 1)

    def relay(sources, g):
        for b in sources:
            for u in range(upper):

                @pl.when(relays(b, u))
                def _():
                    arrived = relay_ref.at[b, u, g]
                    pltpu.make_async_copy(arrived, arrived, relay_recv.at[b, u, g]).wait()
                    second_hop(b, u, g).start()

    def send(g):
        for d in range(dests):

            @pl.when(is_relayed(d, g))
            def _():
                first_hop(d, g).start()

        for d in range(dests):

            @pl.when(is_self(d))
            def _():
                own_copy(d, g).start()

            @pl.when(jnp.logical_not(jnp.logical_or(is_relayed(d, g), is_self(d))))
            def _():
                out_copy(d, g).start()

    step = cols // 2 if cols // 2 % TILE == 0 else TILE

    def lowpass(g):
        def put(at, counts, valid):
            size = counts.shape[0]
            value = gain_ext[pl.ds(at, size)] - jnp.log(
                counts.astype(jnp.float32) - dark_ext[pl.ds(at, size)]
            )
            if valid is not None:
                value = jnp.where(valid, value, 0.0)
            high, low = split(value)
            x_cat[pl.ds(at, size)] = high
            x_cat[pl.ds(ext + at, size)] = low

        put(0, halo_ref[0, g], has[0])
        put(halo, raw_ref[g], None)
        put(halo + rows, halo_ref[1, g], has[1])

        def row_pass(n, carry):
            at = pl.multiple_of(n * step, TILE)
            both = dot(row_band[...], x_cat[:, pl.ds(at, step)])
            high, low = split(both[:rows] + both[rows:])
            to = pl.multiple_of(n * step + LANES, LANES)
            z_high[:, pl.ds(to, step)] = high
            z_low[:, pl.ds(to, step)] = low
            return carry

        lax.fori_loop(0, cols // step, row_pass, 0)

        def windows(z_ref):
            return jnp.concatenate(
                [z_ref[:, n * TILE : (n + 1) * TILE + 2 * LANES] for n in range(tiles)], axis=0
            )

        both = dot(windows(z_high), col_band[...])
        rest = dot(windows(z_low), col_band[:, :TILE])
        value = both[:, :TILE] + (both[:, TILE:] + rest)
        total = jnp.zeros((rows, 1), jnp.float32)
        for n in range(tiles):
            tile = value[n * rows : (n + 1) * rows]
            low_ref[:, n * TILE : (n + 1) * TILE] = tile
            total = total + jnp.sum(tile, axis=1, keepdims=True)
        mean = total * (1.0 / cols)
        for d in range(dests):
            at = d * share
            send_ref[d, g] = (low_ref[pl.ds(at, share)] - mean[at : at + share]).astype(
                jnp.bfloat16
            )

    def relay_inner(g, carry):
        relay(inner, g)
        return carry

    def ready(g):
        return jnp.clip(2 * (g - HOLD), 0, jnp.clip(g, 0, inner_hops))

    def advance(g, carry):
        for side in range(2):

            @pl.when(has[side])
            def _():
                halo_copy(1 - side, g).wait_recv()

        lowpass(g)
        send(g)

        @pl.when(jnp.logical_and(g == 0, EXTRA > 0))
        def _():
            for more in range(EXTRA):
                start_halo(AHEAD + more, True)

        @pl.when(g + AHEAD + EXTRA < planes)
        def _():
            start_halo(g + AHEAD + EXTRA, True)

        each = -(-blocks // (BEHIND - IDLE))
        first = jnp.clip((g - IDLE) * each, 0, blocks)
        final = jnp.clip((g - IDLE + 1) * each, 0, blocks)
        lax.fori_loop(jnp.where(edge, first, blocks), jnp.where(edge, final, blocks), build, 0)

        @pl.when(jnp.logical_and(g > 0, g <= outer_hops))
        def _():
            relay(outer, g - 1)

        lax.fori_loop(ready(g - 1), ready(g), relay_inner, 0)
        return carry

    def arrive(p):
        for a in range(ang_count):
            here = place(a, p)
            pltpu.make_async_copy(here, here, out_recv.at[a, p]).wait()

    def sinogram(p, carry):
        arrive(p)
        count = ang_count * share
        for a in range(ang_count):
            line = lines_ref[a * planes + p].astype(jnp.float32)
            at = pl.ds(pl.multiple_of((a * planes + p) * share, share), share)
            for q in range(cols // LANES):
                x_ref[q, at] = line[:, q * LANES : (q + 1) * LANES]
            for k in range(tiles):
                own = k * count + a * share
                tall_ref[own : own + share] = line[:, k * TILE : (k + 1) * TILE].astype(
                    jnp.bfloat16
                )
        for shift in sorted(range(1 - tiles, tiles), key=abs):
            low, high = max(0, shift), min(tiles, tiles + shift)
            block = strip_ref[(tiles - 1 + shift) * TILE : (tiles + shift) * TILE]
            value = dot(tall_ref[low * count : high * count], block)
            here = pl.ds((low - shift) * count, (high - low) * count)
            if shift:
                acc_ref[here] += value
            else:
                acc_ref[here] = value
        for a in range(ang_count):
            for n in range(tiles):
                own = n * count + a * share
                out_stage[a * planes + p, :, n * TILE : (n + 1) * TILE] = acc_ref[
                    own : own + share
                ].astype(jnp.bfloat16)
            here = a * planes + p
            pltpu.make_async_copy(out_stage.at[here], out_ref.at[here], write_sem.at[a]).start()
        return carry

    pairs = ang_count * planes // 2
    pad = SPAN // LANES
    wide = max(planes // 3, 1)

    def gather(part):
        first, end = part * wide, (part + 1) * wide if part < 2 else planes
        pair(first, end, planes, share, partner_ref, x_ref, left_ref, right_ref)
        for r in range(share):
            product = products(r, first, end, planes, share, left_ref, right_ref)
            if part:
                product = prod_ref[r] + product
            if part < 2:
                prod_ref[r] = product
            else:
                skewed = pltpu.roll(product, 0, 1, stride=1, stride_axis=0)
                prof_ref[pl.ds(r, 1)] = jnp.sum(skewed, axis=0, keepdims=True)[:, LANES:]

    def both(g, carry):
        advance(g, carry)
        sinogram(g - BEHIND, carry)
        return carry

    lax.fori_loop(0, BEHIND, advance, 0)
    lax.fori_loop(BEHIND, planes, both, 0)
    if outer_hops == planes:
        relay(outer, planes - 1)
    lax.fori_loop(ready(planes - 1), inner_hops, relay_inner, 0)
    for v in range(pad):
        right_ref[v] = jnp.zeros(right_ref.shape[1:], jnp.float32)
        right_ref[pad + cols // LANES + v] = jnp.zeros(right_ref.shape[1:], jnp.float32)
    if planes - BEHIND < wide + 2:
        lax.fori_loop(planes - BEHIND, wide + 2, sinogram, 0)
    gather(0)
    lax.fori_loop(max(planes - BEHIND, wide + 2), 2 * wide + 2, sinogram, 0)
    gather(1)
    lax.fori_loop(2 * wide + 2, planes, sinogram, 0)
    gather(2)
    correlate(cols, pairs, shifts_ref, corr_ref, prof_ref)

    for a in range(ang_count):
        here = pl.ds(a * planes, planes)
        pltpu.make_async_copy(out_stage.at[here], out_ref.at[here], write_sem.at[a]).wait()

    for d in range(dests):

        @pl.when(jnp.logical_not(is_self(d)))
        def _():
            sent = send_ref.at[d]
            pltpu.make_async_copy(sent, sent, out_send.at[d]).wait()

    for b in range(row_devices):
        for u in range(upper):

            @pl.when(relays(b, u))
            def _():
                hops = inner_hops if b in inner else outer_hops
                sent = relay_ref.at[b, u, pl.ds(0, hops)]
                pltpu.make_async_copy(sent, sent, relay_send.at[b, u]).wait()

    for side in range(2):

        @pl.when(has[side])
        def _():
            sent = halo_ref.at[side]
            pltpu.make_async_copy(sent, sent, halo_send.at[side]).wait()

    for side in range(2):

        @pl.when(has[side])
        def _():
            for which in range(2):
                level_copy(side, which).wait_send()


def emit_kernel(sino_ref, corr_ref, sino_out, corr_out, sems):
    each = sino_ref.shape[0] // PIECES
    copies = [pltpu.make_async_copy(corr_ref, corr_out, sems.at[PIECES])]
    for n in range(PIECES):
        part = pl.ds(n * each, each)
        copies.append(pltpu.make_async_copy(sino_ref.at[part], sino_out.at[part], sems.at[n]))
    for copy in copies:
        copy.start()
    for copy in copies:
        copy.wait()


def emit(sino, corr):
    hbm = pl.BlockSpec(memory_space=pl.ANY)
    return pl.pallas_call(
        emit_kernel,
        out_shape=(jax.ShapeDtypeStruct(sino.shape, sino.dtype), jax.ShapeDtypeStruct(corr.shape, corr.dtype)),
        in_specs=[hbm, hbm],
        out_specs=(hbm, hbm),
        scratch_shapes=[pltpu.SemaphoreType.DMA((PIECES + 1,))],
        compiler_params=pltpu.CompilerParams(vmem_limit_bytes=2**20),
    )(sino, corr)


def shards(raw_frames, dark_field, flat_field, kernel_taps, partner, shifts):
    planes, rows, cols = raw_frames.shape
    ang_count, row_devices = lax.axis_size("ang"), lax.axis_size("row")
    share = rows // ang_count
    margin = kernel_taps.shape[0] // 2
    halo = -(-margin // 16) * 16
    ext = rows + 2 * halo
    count, half = ang_count * planes, ang_count * planes // 2
    vmem = pl.BlockSpec(memory_space=pltpu.VMEM)
    hbm = pl.BlockSpec(memory_space=pl.ANY)
    bf16, f32 = jnp.bfloat16, jnp.float32
    dma = pltpu.SemaphoreType.DMA
    lines, corr = pl.pallas_call(
        functools.partial(filter_kernel, (ang_count, row_devices, halo)),
        out_shape=(
            jax.ShapeDtypeStruct((count, share, cols), bf16),
            jax.ShapeDtypeStruct((share, shifts.shape[0]), f32),
        ),
        in_specs=[pl.BlockSpec(memory_space=pltpu.HBM)] * 6,
        out_specs=(hbm, vmem),
        scratch_shapes=[
            pltpu.SMEM(kernel_taps.shape, f32),
            pltpu.SMEM(partner.shape, jnp.int32),
            pltpu.VMEM((1,) + shifts.shape, jnp.int32),
            pltpu.VMEM((planes, rows, cols), bf16),
            pltpu.VMEM((rows, cols), bf16),
            pltpu.VMEM((rows, cols), bf16),
            pltpu.VMEM((count, share, cols), bf16),
            pltpu.VMEM((2, planes, halo, cols), bf16),
            pltpu.VMEM((2, 2, halo, cols), bf16),
            pltpu.VMEM((ext, cols), f32),
            pltpu.VMEM((ext, cols), f32),
            pltpu.VMEM((2 * rows, 2 * ext), bf16),
            pltpu.VMEM((TILE + 2 * LANES, 2 * TILE), bf16),
            pltpu.VMEM((2 * ext, cols), bf16),
            pltpu.VMEM((rows, cols + 2 * LANES), bf16),
            pltpu.VMEM((rows, cols + 2 * LANES), bf16),
            pltpu.VMEM((rows, cols), f32),
            pltpu.VMEM((ang_count, planes, share, cols), bf16),
            pltpu.VMEM((row_devices, ang_count // row_devices, planes, share, cols), bf16),
            pltpu.VMEM((2 * cols - TILE, TILE), bf16),
            pltpu.VMEM((cols // LANES, count * share, LANES), f32),
            pltpu.VMEM((cols // LANES, half * share, LANES), f32),
            pltpu.VMEM(((cols + 2 * SPAN) // LANES, half * share, LANES), f32),
            pltpu.VMEM((share, LANES, 2 * SPAN + LANES), f32),
            pltpu.VMEM((share, 2 * SPAN), f32),
            pltpu.VMEM((cols // TILE * ang_count * share, TILE), bf16),
            pltpu.VMEM((cols // TILE * ang_count * share, TILE), f32),
            pltpu.VMEM((count, share, cols), bf16),
            dma((planes,)),
            dma((5,)),
            dma((ang_count,)),
            dma((2, 2)),
            dma((2, 2)),
            dma((2,)),
            dma((2, planes)),
            dma((ang_count,)),
            dma((ang_count, planes)),
            dma((row_devices, ang_count // row_devices)),
            dma((row_devices, ang_count // row_devices, planes)),
        ],
        compiler_params=pltpu.CompilerParams(collective_id=0, has_side_effects=True, vmem_limit_bytes=40 * 2**20),
    )(*(pltpu.with_memory_space_constraint(v, pltpu.HBM) for v in (kernel_taps, raw_frames, dark_field, flat_field, partner, shifts[None])))
    return emit(lines, corr)


def solution(mesh):
    in_specs = (
        P(("scan", "ang"), "row", None),
        P("row", None),
        P("row", None),
        P(),
        P("scan"),
        P(),
    )
    out_specs = (P("scan", ("ang", "row"), None), P(("scan", "ang", "row"), None))
    return jax.shard_map(shards, mesh=mesh, in_specs=in_specs, out_specs=out_specs, check_vma=False)
```
